32 devices in a mesh: seq: 8 (over y, x, core), tp: 4 (over z).
Axes of the slice: x: 2, y: 2, z: 4, core: 2. Of those that a mesh axis runs over, the one named last changes fastest.
Arguments:
- tokens: bfloat16 [1, 8, 1024, 768], P(None, 'seq', 'tp'), may hold values from -6 to 6
- cotangent: bfloat16 [1, 8, 1024, 768], P(None, 'seq', 'tp'), may hold values from -6 to 6
- lengths: int32 [1], replicated, may hold values from 64 to 1024
- column_mask: int32 [1, 1024], replicated, may hold values 0 or 1
- row_gain: float32 [768], replicated, may hold values from 0.5 to 1.5
- row_qkv: bfloat16 [3, 768, 768], P(None, None, 'tp'), may hold values from -0.3125 to 0.3125
- row_out: bfloat16 [768, 768], P('tp'), may hold values from -0.625 to 0.625
- col_gain: float32 [768], replicated, may hold values from 0.5 to 1.5
- col_qkv: bfloat16 [3, 768, 768], P(None, None, 'tp'), may hold values from -0.21875 to 0.21875
- col_out: bfloat16 [768, 768], P('tp'), may hold values from -0.875 to 0.875
- ffn_gain: float32 [768], replicated, may hold values from 0.5 to 1.5
- ffn_up: bfloat16 [768, 3072], P(None, 'tp'), may hold values from -0.21875 to 0.21875
- ffn_down: bfloat16 [3072, 768], P('tp'), may hold values from -0.109375 to 0.109375
Outputs:
- activations: bfloat16 [1, 8, 1024, 768], P(None, 'seq', 'tp')
- input_grad: bfloat16 [1, 8, 1024, 768], P(None, 'seq', 'tp')
- row_gain_grad: float32 [768], replicated
- row_qkv_grad: float32 [3, 768, 768], P(None, 'seq', 'tp')
- row_out_grad: float32 [768, 768], P('tp', 'seq')
- col_gain_grad: float32 [768], replicated
- col_qkv_grad: float32 [3, 768, 768], P(None, 'seq', 'tp')
- col_out_grad: float32 [768, 768], P('tp', 'seq')
- ffn_gain_grad: float32 [768], replicated
- ffn_up_grad: float32 [768, 3072], P('seq', 'tp')
- ffn_down_grad: float32 [3072, 768], P('tp', 'seq')
The draws below stay inside these ranges and needn't reach their ends.
All inputs are finite; a program needn't handle non-finite values.
Results may differ from the reference program's by a relative error of at most 0.025.
The reference program's roundings to bfloat16 on the way count: a program that leaves them out, or rounds other values in their place, can miss the bound.
Values may be sent and summed in bfloat16 or wider, within the bound.
No kernel may reach another device: no remote copies, remote signals or barrier semaphores. Data moves between devices by JAX's collectives and lax.ppermute only.
A program may use at most 192 MiB of HBM per device.

```python
import math
import jax
import jax.numpy as jnp
from jax import lax

D = 768
HEADS = 12
HEAD = 64
FF = 3072
ALIGNS = 1
COLS = 1024
SEQS = 8


def set_ends(entries, own_key, least, high):
    shape = entries.shape
    place = [jax.random.randint(jax.random.fold_in(own_key, axis), (), 0, shape[axis]) for axis in range(len(shape))]
    entries = entries.at[tuple(place)].set(least)
    longest = shape.index(max(shape))
    place[longest] = (place[longest] + 1) % shape[longest]
    return entries.at[tuple(place)].set(high)


def steps_of(rng, dims, cuts, smallest, top_value):
    gain, own = 1.0, jax.random.fold_in(rng, 6)
    for axis_at, parts in cuts:
        heights = jnp.exp(jax.random.uniform(jax.random.fold_in(own, axis_at), (parts,), jnp.float32, smallest / len(cuts), top_value / len(cuts)))
        gain = gain * jnp.repeat(heights, dims[axis_at] // parts).reshape([-1 if axis == axis_at else 1 for axis in range(len(dims))])
    return gain


def scatter_about(own_key, shape, deviation, bound, cuts=(), kind=jnp.bfloat16):
    drawn = jax.random.normal(own_key, shape, jnp.float32) * deviation
    if len(cuts) > 0:
        drawn = steps_of(own_key, shape, cuts, -0.22, 0.18) * drawn
    return jnp.clip(drawn, min=-bound, max=bound).astype(kind)


def setup_inputs(seed: int = 0) -> dict:
    arg_keys = jax.random.split(jax.random.key(seed), 14)
    return {
        "tokens": scatter_about(arg_keys[0], (ALIGNS, SEQS, COLS, D), 1.0, 6.0, ((1, 8), (2, 4))),
        "cotangent": scatter_about(arg_keys[1], (ALIGNS, SEQS, COLS, D), 1.0, 6.0, ((1, 8), (2, 4))),
        "lengths": jax.random.randint(arg_keys[2], (ALIGNS,), COLS // 16, COLS + 1).astype(jnp.int32),
        "column_mask": set_ends((jax.random.randint(arg_keys[3], (ALIGNS, COLS), 0, 8) < 7).astype(jnp.int32), jax.random.fold_in(arg_keys[3], 1), 0, 1),
        "row_gain": jnp.clip(1.0 + 0.1 * jax.random.normal(arg_keys[4], (D,), jnp.float32), 0.5, 1.5),
        "row_qkv": scatter_about(arg_keys[5], (3, D, D), (D // 2) ** -0.5, 0.3125, ((2, 4),)),
        "row_out": scatter_about(arg_keys[6], (D, D), (D // 8) ** -0.5, 0.625, ((0, 4),)),
        "col_gain": jnp.clip(1.0 + 0.1 * jax.random.normal(arg_keys[7], (D,), jnp.float32), 0.5, 1.5),
        "col_qkv": scatter_about(arg_keys[8], (3, D, D), D ** -0.5, 0.21875, ((2, 4),)),
        "col_out": scatter_about(arg_keys[9], (D, D), (D // 16) ** -0.5, 0.875, ((0, 4),)),
        "ffn_gain": jnp.clip(1.0 + 0.1 * jax.random.normal(arg_keys[10], (D,), jnp.float32), 0.5, 1.5),
        "ffn_up": scatter_about(arg_keys[11], (D, FF), D ** -0.5, 0.21875, ((1, 4),)),
        "ffn_down": scatter_about(arg_keys[12], (FF, D), FF ** -0.5, 0.109375, ((0, 4),)),
    }


@jax.custom_vjp
def lowered_input(v):
    return lax.optimization_barrier(v.astype(jnp.bfloat16)).astype(jnp.float32)

@jax.custom_vjp
def lowered_gradient(v):
    return v

def low_keep(v):
    return (lowered_input(v), None)

def low_pass(kept, grad):
    return (grad,)

def back_keep(v):
    return (v, None)

def back_low(kept, grad):
    return (lowered_input(grad),)
lowered_input.defvjp(low_keep, low_pass)
lowered_gradient.defvjp(back_keep, back_low)
EPSILON = 1e-05
NEGATIVE = -1e+30
ENTROPY_WEIGHT = 4.0
EXACT_PRECISION = lax.Precision.HIGHEST

def layer_norm(skip_carry_tensor, norm_gain):
    average = lax.optimization_barrier(jnp.mean(skip_carry_tensor, axis=-1, keepdims=True))
    centred = skip_carry_tensor - average
    spread = lax.optimization_barrier(jnp.mean(centred * centred, axis=-1, keepdims=True))
    return centred * lax.rsqrt(spread + EPSILON) * norm_gain

def row_block(skip_carry_tensor, norm_gain, query_key_value_weight, output_weight, target_present_flags, source_present_flags, penalty_scale):
    seq_count = skip_carry_tensor.shape[0]
    normed_input = lowered_input(layer_norm(skip_carry_tensor, norm_gain))
    projected_output = lowered_gradient(lowered_input(jnp.einsum('bwo,iof->ibwf', normed_input, query_key_value_weight, precision=EXACT_PRECISION)))
    heads = projected_output.reshape(3, seq_count, COLS, HEADS, HEAD)
    logits = jnp.einsum('sihe,sjhe->hij', heads[0], heads[1], precision=EXACT_PRECISION) * (HEAD * SEQS) ** (-0.5)
    logits = lowered_gradient(logits)
    key_ok = target_present_flags[None, None, :]
    masked = jnp.where(key_ok, logits, NEGATIVE)
    row_top = lax.optimization_barrier(jnp.max(masked, axis=-1, keepdims=True))
    powers = jnp.exp(masked - row_top)
    row_total = lax.optimization_barrier(jnp.sum(powers, axis=-1, keepdims=True))
    probs = powers / row_total
    entropy = (row_top + jnp.log(row_total))[..., 0] - lax.optimization_barrier(jnp.sum(jnp.where(key_ok, probs * masked, 0.0), axis=-1))
    penalty = penalty_scale * jnp.sum(jnp.where(source_present_flags[None, :], entropy, 0.0))
    attended_output = jnp.einsum('hij,sjhe->sihe', lowered_input(probs), heads[2], precision=EXACT_PRECISION)
    attended_output = lowered_gradient(lowered_input(attended_output.reshape(seq_count, COLS, D)))
    branch_output = lowered_gradient(jnp.einsum('wxf,fh->wxh', attended_output, output_weight, precision=EXACT_PRECISION))
    return (skip_carry_tensor + branch_output, penalty)

def col_block(skip_carry_tensor, norm_gain, query_key_value_weight, output_weight):
    seq_count = skip_carry_tensor.shape[0]
    normed_input = lowered_input(layer_norm(skip_carry_tensor, norm_gain))
    projected_output = lowered_gradient(lowered_input(jnp.einsum('bwo,iof->ibwf', normed_input, query_key_value_weight, precision=EXACT_PRECISION)))
    heads = projected_output.reshape(3, seq_count, COLS, HEADS, HEAD)
    scores = lowered_gradient(jnp.einsum('sjhe,tjhe->jhst', heads[0], heads[1], precision=EXACT_PRECISION) * HEAD ** (-0.5))
    column_upper_bound = lax.optimization_barrier(jnp.max(scores, axis=-1, keepdims=True))
    powers = jnp.exp(scores - column_upper_bound)
    probs = powers / lax.optimization_barrier(jnp.sum(powers, axis=-1, keepdims=True))
    attended_output = jnp.einsum('jhst,tjhe->sjhe', lowered_input(probs), heads[2], precision=EXACT_PRECISION)
    attended_output = lowered_gradient(lowered_input(attended_output.reshape(seq_count, COLS, D)))
    return skip_carry_tensor + lowered_gradient(jnp.einsum('wxf,fh->wxh', attended_output, output_weight, precision=EXACT_PRECISION))

def ffn_block(skip_carry_tensor, norm_gain, up_weight, down_weight):
    seq_count = skip_carry_tensor.shape[0]
    block_size = math.gcd(seq_count * COLS, 4096)
    flattened = skip_carry_tensor.reshape(-1, block_size, D)

    def one_block(attention_contents):
        normed_input = lowered_input(layer_norm(attention_contents, norm_gain))
        hidden_pre = lowered_gradient(jnp.einsum('td,df->tf', normed_input, up_weight, precision=EXACT_PRECISION))
        hidden = lowered_input(jax.nn.gelu(hidden_pre, approximate=False))
        return attention_contents + lowered_gradient(jnp.einsum('tf,fd->td', hidden, down_weight, precision=EXACT_PRECISION))
    return lax.map(jax.checkpoint(one_block), flattened).reshape(seq_count, COLS, D)

def reference(tokens, cotangent, lengths, column_mask, row_gain, row_qkv, row_out, col_gain, col_qkv, col_out, ffn_gain, ffn_up, ffn_down):
    position = jnp.arange(COLS, dtype=jnp.int32)
    target_present_flags = (position[None, :] < lengths[:, None]) & ((column_mask == 1) | (position[None, :] == 0))
    source_present_flags = position[None, :] < lengths[:, None]
    penalty_scale = ENTROPY_WEIGHT * (ALIGNS * SEQS * COLS) / (HEADS * jnp.sum(lengths).astype(jnp.float32))

    def forward(skip_carry_tensor, row_norm, row_weight, row_mix, col_norm, col_weight, col_mix, ffn_norm, up_weight, down_weight):

        def protein_family_matrix(packed):
            attention_contents, keys_valid, queries_valid = packed
            attention_contents, penalty = row_block(attention_contents, row_norm, row_weight, row_mix, keys_valid, queries_valid, penalty_scale)
            attention_contents = col_block(attention_contents, col_norm, col_weight, col_mix)
            attention_contents = ffn_block(attention_contents, ffn_norm, up_weight, down_weight)
            return (attention_contents, penalty)
        block_returns, disorder_charges = lax.map(jax.checkpoint(protein_family_matrix), (skip_carry_tensor, target_present_flags, source_present_flags))
        return (block_returns, jnp.sum(disorder_charges))
    (block_returns, penalty_total), pullback = jax.vjp(forward, tokens.astype(jnp.float32), row_gain, row_qkv.astype(jnp.float32), row_out.astype(jnp.float32), col_gain, col_qkv.astype(jnp.float32), col_out.astype(jnp.float32), ffn_gain, ffn_up.astype(jnp.float32), ffn_down.astype(jnp.float32))
    grads = pullback((cotangent.astype(jnp.float32), jnp.ones((), jnp.float32)))
    return (block_returns.astype(jnp.bfloat16), grads[0].astype(jnp.bfloat16), grads[1], grads[2], grads[3], grads[4], grads[5], grads[6], grads[7], grads[8], grads[9])
```

```python
import functools

import jax
import jax.numpy as jnp
from jax import lax
from jax.experimental import pallas as pl
from jax.experimental.pallas import tpu as pltpu
from jax.sharding import Mesh
from jax.sharding import PartitionSpec as P

HEADS = 12
HEAD = 64
EPSILON = 1e-05
NEGATIVE = -1e30
ENTROPY_WEIGHT = 4.0

SEQ = ("c", "r")
BF = jnp.bfloat16
F32 = jnp.float32
VMEM_LIMIT = 60 * 1024 * 1024


def statistics(value):
    average = jnp.mean(value, axis=-1, keepdims=True)
    centred = value - average
    inverse = lax.rsqrt(jnp.mean(centred * centred, axis=-1, keepdims=True) + EPSILON)
    return centred * inverse, inverse


def layer_norm(value, gain):
    unit, _ = statistics(value)
    return unit * gain


def norm_back(value, gain, upstream):
    unit, inverse = statistics(value)
    scaled = upstream * gain
    back = inverse * (
        scaled
        - jnp.mean(scaled, axis=-1, keepdims=True)
        - unit * jnp.mean(scaled * unit, axis=-1, keepdims=True)
    )
    return back, jnp.sum(upstream * unit, axis=0, keepdims=True)


def gelu_parts(value):
    share = 0.5 * (1.0 + lax.erf(value * (0.5**0.5)))
    slope = share + value * jnp.exp(-0.5 * value * value) * 0.3989422804014327
    return value * share, slope


def mm(left, right):
    return lax.dot_general(left, right, (((1,), (0,)), ((), ())), preferred_element_type=F32)


def mm_nt(left, right):
    return lax.dot_general(left, right, (((1,), (1,)), ((), ())), preferred_element_type=F32)


def swap(value, axis, size, mask):
    return lax.ppermute(value, axis, [(i, i ^ mask) for i in range(size)])


def bits_of(size):
    return [1 << b for b in range(size.bit_length() - 1)]


def exchange(value, axis):
    return lax.all_to_all(value, axis, split_axis=0, concat_axis=0, tiled=True)


ANY = pl.BlockSpec(memory_space=pl.ANY)
VMEM = pl.BlockSpec(memory_space=pltpu.VMEM)
SMEM = pl.BlockSpec(memory_space=pltpu.SMEM)


def call(body, outs, *args, specs=None, scratch=(), flops=0, moved=0):
    inner = body.func if isinstance(body, functools.partial) else body
    cost = pl.CostEstimate(flops=int(flops), bytes_accessed=int(moved), transcendentals=0)
    return pl.pallas_call(
        body,
        out_shape=[jax.ShapeDtypeStruct(shape, kind) for shape, kind in outs],
        in_specs=[VMEM] * len(args) if specs is None else specs,
        out_specs=[VMEM] * len(outs),
        scratch_shapes=list(scratch),
        compiler_params=pltpu.CompilerParams(vmem_limit_bytes=VMEM_LIMIT),
        cost_estimate=cost if flops else None,
        name=inner.__name__,
    )(*args)


def fetch(me_ref, tp, shard, parts, store, sems):
    copies = [[pltpu.make_async_copy(shard, store.at[0], sems.at[0, 0])]]
    for k in range(1, tp):
        if len(parts) == 1:
            source = parts[0].at[me_ref[1] ^ k]
            copies.append([pltpu.make_async_copy(source, store.at[k], sems.at[k, 0])])
        else:
            copies.append(
                [
                    pltpu.make_async_copy(
                        part.at[k - 1], store.at[k, me_ref[0] ^ m], sems.at[k, m]
                    )
                    for m, part in enumerate(parts)
                ]
            )
    for group in copies:
        for copy in group:
            copy.start()

    def wait(k):
        for copy in copies[k]:
            copy.wait()

    return wait


def relative_rows(me_ref, order, turned, store):
    if order is None:
        return turned
    store[...] = turned
    rows = turned.shape[0] >> len(order)
    picked = []
    for m in range(1 << len(order)):
        mask = sum(((m >> (len(order) - 1 - i)) & 1) << bit for i, bit in enumerate(order))
        start = pl.multiple_of((me_ref[0] ^ mask) * rows, rows)
        picked.append(store[pl.ds(start, rows), :])
    return jnp.concatenate(picked, axis=0)


def store_rows(me_ref, order, refs, k, columns, value):
    if order is None:
        refs[0][me_ref[1] ^ k, :, columns] = value
        return
    half = value.shape[0] // 2
    for ref, part in zip(refs, (value[:half], value[half:])):
        ref[:, k, :, columns] = part.reshape(ref.shape[0], ref.shape[2], -1)


def project(dims, me_ref, *refs):
    slots, ranks, few, tp, heads = dims
    blocks, (gain, weight, normed, pieces) = refs[:tp], refs[tp:]
    features = heads * HEAD
    part = slots * few
    pieces[heads * ranks :] = jnp.zeros_like(pieces[heads * ranks :])
    for k in range(tp):
        z = me_ref[1] ^ k
        value = blocks[k][...].astype(F32).reshape(slots, ranks, few, -1)
        value = jnp.concatenate(
            [value[c, r] for r in range(ranks) for c in range(slots)], axis=0
        )
        low = layer_norm(value, gain[...]).astype(BF)
        normed[z] = low
        columns = pl.ds(pl.multiple_of(z * part, part), part)
        proj = mm_nt(weight[...], low).astype(BF)
        for c in range(heads):
            for r in range(ranks):
                for t in range(3):
                    rows = t * features + c * HEAD
                    piece = proj[rows : rows + HEAD, r * part : (r + 1) * part]
                    pieces[c * ranks + r, t, :, columns] = piece


def tied_softmax(own, other, key_ok, scale):
    depth = own.shape[0] * own.shape[2]
    turned = own[:, 0].reshape(depth, -1).T
    logits = jnp.concatenate(
        [mm(turned, pair[:, 1].reshape(depth, -1)) for pair in (own, other)], axis=1
    )
    ok = key_ok[...] > 0
    masked = jnp.where(ok, logits * scale, NEGATIVE)
    powers = jnp.exp(masked - jnp.max(masked, axis=-1, keepdims=True))
    return masked, powers * (1.0 / jnp.sum(powers, axis=-1, keepdims=True)), ok


def attend(scale, own, other, key_ok, mixed):
    _, probs, _ = tied_softmax(own, other, key_ok, scale)
    depth = own.shape[0] * own.shape[2]
    low = probs.astype(BF)
    half = low.shape[1] // 2
    total = mm_nt(low[:, :half], own[:, 2].reshape(depth, -1))
    total += mm_nt(low[:, half:], other[:, 2].reshape(depth, -1))
    mixed[...] = total.astype(BF).reshape(mixed.shape)


def attend_back(scale, own, other, key_ok, weight, mixed_grad, query_grad, kept, given):
    masked, probs, ok = tied_softmax(own, other, key_ok, scale)
    seqs = own.shape[0]
    depth = seqs * own.shape[2]
    low = probs.astype(BF)
    half = low.shape[1] // 2
    out_grad = mixed_grad[...].reshape(-1, depth)
    prob_grad = jnp.concatenate(
        [mm(out_grad, pair[:, 2].reshape(depth, -1)) for pair in (own, other)], axis=1
    )
    prob_dot = jnp.sum(probs * prob_grad, axis=-1, keepdims=True)
    mean_logit = jnp.sum(jnp.where(ok, probs * masked, 0.0), axis=-1, keepdims=True)
    entropy = jnp.where(ok, probs * (masked - mean_logit), 0.0)
    grad = (probs * (prob_grad - prob_dot) - weight[...] * entropy).astype(BF)
    total = mm_nt(own[:, 1].reshape(depth, -1), grad[:, :half])
    total += mm_nt(other[:, 1].reshape(depth, -1), grad[:, half:])
    query_grad[...] = (total * scale).astype(BF).reshape(query_grad.shape)
    turned = out_grad.T
    flat = own[:, 0].reshape(depth, -1)
    shape = (seqs, HEAD, half)
    given[:, 0] = (mm(flat, grad[:, half:]) * scale).astype(BF).reshape(shape)
    given[:, 1] = mm(turned, low[:, half:]).astype(BF).reshape(shape)
    kept[:, 0] = (mm(flat, grad[:, :half]) * scale).reshape(shape)
    kept[:, 1] = mm(turned, low[:, :half]).reshape(shape)


def column_probs(query, key, rule, scale):
    scores = jnp.where(rule, mm_nt(query, key) * scale, NEGATIVE)
    powers = jnp.exp(scores - jnp.max(scores, axis=-1, keepdims=True))
    return powers * (1.0 / jnp.sum(powers, axis=-1, keepdims=True))


def same_column(count, few):
    rows = lax.broadcasted_iota(jnp.int32, (count, count), 0)
    columns = lax.broadcasted_iota(jnp.int32, (count, count), 1)
    return (rows % few) == (columns % few)


def narrow(store, k, features):
    whole = store[k].reshape(-1, store.shape[3])
    return [whole[i * features : (i + 1) * features] for i in range(5)]


def columns_forward(dims, parts, me_ref, tokens, attended, gain, shard, *refs):
    few, tp, heads = dims
    parts, (after_row, normed, proj, mixed, after_col, store, sems) = refs[:parts], refs[parts:]
    wait = fetch(me_ref, tp, shard, parts, store, sems)
    features = heads * HEAD
    count = tokens.shape[0]
    total = tokens[...].astype(F32)

    update = jnp.zeros_like(total)
    for k in range(tp):
        wait(k)
        update += mm(attended[me_ref[1] ^ k], narrow(store, k, features)[0])
    total = total + update
    after_row[...] = total
    low = layer_norm(total, gain[...]).astype(BF)
    normed[...] = low
    rule = same_column(count, few)
    update = jnp.zeros_like(total)
    for k in range(tp):
        weights = narrow(store, k, features)
        for t in range(3):
            proj[t, k] = mm_nt(low, weights[2 + t]).astype(BF)
        for h in range(heads):
            at = slice(h * HEAD, (h + 1) * HEAD)
            probs = column_probs(proj[0, k, :, at], proj[1, k, :, at], rule, HEAD**-0.5)
            mixed[k, :, at] = mm(probs.astype(BF), proj[2, k, :, at]).astype(BF)
        update += mm(mixed[k], weights[1])
    after_col[...] = total + update


def columns_backward(dims, parts, order, me_ref, *refs):
    few, tp, heads = dims
    middle, after_row, normed, proj, mixed, attended, gain, shard = refs[:8]
    parts, refs = refs[8 : 8 + parts], refs[8 + parts :]
    inner, inner_low, row_mixed, gain_grad = refs[:4]
    grads, (col_grad, rows, store, sems) = refs[4:-4], refs[-4:]
    wait = fetch(me_ref, tp, shard, parts, store, sems)
    features = heads * HEAD
    count = middle.shape[0]
    middle_low = middle[...].astype(BF)
    turned = relative_rows(me_ref, order, middle_low.T, rows)
    normed_turned = relative_rows(me_ref, order, normed[...].T, rows)
    rule = same_column(count, few)
    upstream = jnp.zeros(middle.shape, F32)
    for k in range(tp):
        wait(k)
        weights = narrow(store, k, features)
        mixed_grad = mm_nt(middle_low, weights[1]).astype(BF)
        for h in range(heads):
            at = slice(h * HEAD, (h + 1) * HEAD)
            query, key, value = proj[0, k, :, at], proj[1, k, :, at], proj[2, k, :, at]
            probs = column_probs(query, key, rule, HEAD**-0.5)
            out_grad = mixed_grad[:, at]
            prob_grad = mm_nt(out_grad, value)
            score = probs * (prob_grad - jnp.sum(probs * prob_grad, axis=-1, keepdims=True))
            score = score.astype(BF)
            col_grad[0, :, at] = (mm(score, key) * HEAD**-0.5).astype(BF)
            col_grad[1, :, at] = (mm(score.T, query) * HEAD**-0.5).astype(BF)
            col_grad[2, :, at] = mm(probs.astype(BF).T, out_grad).astype(BF)
        pieces = []
        for t in range(3):
            upstream += mm(col_grad[t], weights[2 + t])
            pieces.append(mm(normed_turned, col_grad[t]).astype(BF))
        pieces.append(mm(turned, mixed[k]).astype(BF))
        store_rows(
            me_ref, order, grads, k, slice(0, 4 * features), jnp.concatenate(pieces, axis=1)
        )
    back, gain_grad[...] = norm_back(after_row[...], gain[...], upstream)
    total = middle[...] + back
    inner[...] = total
    low = total.astype(BF)
    inner_low[...] = low
    turned = relative_rows(me_ref, order, low.T, rows)
    for k in range(tp):
        z = me_ref[1] ^ k
        value = mm(turned, attended[z]).astype(BF)
        store_rows(me_ref, order, grads, k, slice(4 * features, 5 * features), value)
        row_mixed[z] = mm_nt(low, narrow(store, k, features)[0]).astype(BF)


def feed_forward(tp, parts, orders, me_ref, after_col, cotangent, gain, up_shard, down_shard, *refs):
    parts, refs = refs[:parts], refs[parts:]
    outputs, middle, gain_grad = refs[:3]
    grads, (rows, store, sems) = refs[3:-3], refs[-3:]
    count = len(grads) // 2
    half = store.shape[1] // 2
    own_up = pltpu.make_async_copy(up_shard, store.at[0, :half], sems.at[0, 0])
    own_down = pltpu.make_async_copy(down_shard, store.at[0, half:], sems.at[0, 1])
    copies = [[own_up, own_down]]
    for k in range(1, tp):
        if len(parts) == 1:
            source = parts[0].at[me_ref[1] ^ k]
            copies.append([pltpu.make_async_copy(source, store.at[k], sems.at[k, 0])])
        else:
            copies.append(
                [
                    pltpu.make_async_copy(
                        part.at[k - 1], store.at[k, me_ref[0] ^ m], sems.at[k, m]
                    )
                    for m, part in enumerate(parts)
                ]
            )
    for group in copies:
        for copy in group:
            copy.start()
    value = after_col[...]
    low = layer_norm(value, gain[...]).astype(BF)
    given = cotangent[...]
    low_turned = relative_rows(me_ref, orders[0], low.T, rows)
    given_turned = relative_rows(me_ref, orders[1], given.T, rows)
    result = value
    upstream = jnp.zeros_like(value)
    for k in range(tp):
        for copy in copies[k]:
            copy.wait()
        up = store[k, :half].reshape(-1, store.shape[3])
        down = store[k, half:].reshape(-1, store.shape[3])
        hidden, slope = gelu_parts(mm(low, up))
        hidden = hidden.astype(BF)
        result += mm(hidden, down)
        pre_grad = (mm_nt(given, down) * slope).astype(BF)
        upstream += mm_nt(pre_grad, up)
        everything = slice(0, up.shape[1])
        value_up = mm(low_turned, pre_grad).astype(BF)
        store_rows(me_ref, orders[0], grads[:count], k, everything, value_up)
        value_down = mm(given_turned, hidden).astype(BF)
        store_rows(me_ref, orders[1], grads[count:], k, everything, value_down)
    outputs[...] = result.astype(BF)
    back, gain_grad[...] = norm_back(value, gain[...], upstream)
    middle[...] = given.astype(F32) + back


def gather_grads(dims, order, me_ref, pieces_in, normed, gain, weight, *outs):
    slots, ranks, few, tp, heads = dims
    features = heads * HEAD
    part = slots * few
    pieces, (kept, sent, gain_grad, rows) = outs[:tp], outs[tp:]
    total = jnp.zeros((3 * features, normed.shape[2]), F32)
    for k in range(tp):
        z = me_ref[1] ^ k
        columns = pl.ds(pl.multiple_of(z * part, part), part)
        for c in range(heads):
            for r in range(ranks):
                for t in range(3):
                    piece = pieces_in[c * ranks + r, t, :, columns]
                    at = t * features + c * HEAD
                    pieces[k][at : at + HEAD, r * part : (r + 1) * part] = piece
        total += mm(pieces[k][...], normed[z])
    gain_grad[...] = (
        jnp.sum(total * weight[...].astype(F32), axis=0, keepdims=True) / gain[...]
    )
    turned = relative_rows(me_ref, order, total.T.astype(BF), rows)
    half = turned.shape[0] // 2
    kept[...] = turned[:half].reshape(kept.shape)
    sent[...] = turned[half:].reshape(sent.shape)


def finish(dims, parts, me_ref, *refs):
    slots, ranks, few, tp, heads = dims
    features = heads * HEAD
    pieces, refs = refs[:tp], refs[tp:]
    tokens, gain, inner, shard = refs[:4]
    parts, (result, store, sems) = refs[4 : 4 + parts], refs[4 + parts :]
    wait = fetch(me_ref, tp, shard, parts, store, sems)
    upstream = jnp.zeros(inner.shape, F32)
    for k in range(tp):
        wait(k)
        whole = store[k].reshape(-1, store.shape[3])[: 3 * features]
        upstream += mm(pieces[k][...].T, whole)
    upstream = upstream.reshape(ranks, slots, few, -1)
    upstream = jnp.concatenate(
        [upstream[r, c] for c in range(slots) for r in range(ranks)], axis=0
    )
    back, _ = norm_back(tokens[...].astype(F32), gain[...], upstream)
    result[...] = (inner[...].astype(F32) + back).astype(BF)


def after(value, *others):
    return lax.optimization_barrier((value,) + others)[0]


def add(left, right):
    return (left.astype(F32) + right.astype(F32)).astype(BF)


def local(
    tokens,
    cotangent,
    lengths,
    column_mask,
    row_gain,
    row_qkv,
    row_out,
    col_gain,
    col_qkv,
    col_out,
    ffn_gain,
    ffn_up,
    ffn_down,
):
    slots, ranks, tp = lax.axis_size("c"), lax.axis_size("r"), lax.axis_size("tp")
    seqs = slots * ranks
    block, width = tokens.shape[2], tokens.shape[3]
    cols = column_mask.shape[1]
    few = block // seqs
    part = slots * few
    features = row_qkv.shape[2]
    heads = features // HEAD
    hidden = ffn_up.shape[1]
    queries = tp * part
    count = seqs * few
    tied_scale = (HEAD * seqs) ** (-0.5)
    my_seq, my_rank, my_z = lax.axis_index(SEQ), lax.axis_index("r"), lax.axis_index("tp")
    me_ref = jnp.stack([my_seq, my_z]).astype(jnp.int32)
    dims = (slots, ranks, few, tp, heads)
    fast = seqs == 8 and ranks == 2
    row_gain, col_gain, ffn_gain = row_gain[None], col_gain[None], ffn_gain[None]

    penalty_scale = ENTROPY_WEIGHT * (seqs * cols) / (HEADS * jnp.sum(lengths).astype(F32))
    position = jnp.arange(cols, dtype=jnp.int32).reshape(tp, slots, ranks, few)
    position = position.transpose(2, 0, 1, 3)
    flag = column_mask.reshape(tp, slots, ranks, few).transpose(2, 0, 1, 3)
    valid = (position < lengths[0]) & ((flag == 1) | (position == 0))
    valid = valid.astype(F32).reshape(ranks, queries)
    key_ok = jnp.concatenate(
        [lax.dynamic_index_in_dim(valid, my_rank ^ k, 0) for k in range(ranks)], axis=1
    )
    query_position = lax.dynamic_index_in_dim(position.reshape(ranks, queries), my_rank, 0)
    query_weight = jnp.where(query_position < lengths[0], penalty_scale, 0.0).reshape(queries, 1)

    own = tokens[0, 0]
    blocks = [own] + [swap(own, "tp", tp, k) for k in range(1, tp)]
    residual = exchange(own.reshape(seqs, few, width), SEQ).reshape(count, width)
    given = exchange(cotangent[0, 0].reshape(seqs, few, width), SEQ).reshape(count, width)

    row_weight = row_qkv.transpose(0, 2, 1).reshape(3 * features, width)
    shard_a = jnp.concatenate(
        [row_out, col_out, col_qkv.transpose(0, 2, 1).reshape(3 * features, width)]
    )

    def cut(shard, least):
        rows = shard.shape[0]
        rows += -rows % (seqs * least)
        shard = jnp.pad(shard, ((0, rows - shard.shape[0]), (0, 0)))
        return shard.reshape(seqs, rows // seqs, width)

    shard_a = cut(shard_a, 16 if fast else 1)
    shard_c = cut(row_weight, 16 if fast else 1)
    shard_b = cut(jnp.concatenate([ffn_up, ffn_down]), 1)

    def mine(shard):
        return lax.dynamic_index_in_dim(shard, my_seq, 0, keepdims=False)

    def along_tp(piece):
        return jnp.stack([swap(piece, "tp", tp, k) for k in range(1, tp)])

    def along_seq(held, masks, gate=None):
        first = swap(held, "c", slots, masks[0])
        second = [swap(p, "c", slots, masks[1]) for p in (held, first)]
        by_slot = {0: held, masks[0]: first, masks[1]: second[0], masks[0] ^ masks[1]: second[1]}
        by_slot = [by_slot[c] for c in range(4)]
        return [p for q in by_slot for p in (q, swap(q, "r", ranks, 1))]

    if fast:
        piece_a = after(mine(shard_a), *blocks[1:])
        near_a = along_tp(piece_a)
        near_b = along_tp(after(mine(shard_b), near_a))
        parts_a = along_seq(near_a, (1, 2))
        parts_b = along_seq(near_b, (2, 1))
        near_c = along_tp(after(mine(shard_c), *parts_b))
        parts_c = along_seq(near_c, (1, 2))
        blocks[1] = after(blocks[1], residual, given)
    else:

        def everywhere(shard):
            rows = shard.shape[0] * shard.shape[1]
            whole = lax.all_gather(mine(shard), ("tp",) + SEQ, axis=0)
            return [whole.reshape(tp, 8, rows // 8, width)]

        parts_a, parts_b, parts_c = everywhere(shard_a), everywhere(shard_b), everywhere(shard_c)
        shard_a = shard_a.reshape(8, -1, width)
        shard_c = shard_c.reshape(8, -1, width)
    up_own = ffn_up.reshape(4, -1, width)
    down_own = ffn_down.reshape(4, -1, width)
    store_a = pltpu.VMEM((tp,) + shard_a.shape, BF)
    store_b = pltpu.VMEM((tp, 8, shard_b.shape[0] * shard_b.shape[1] // 8, width), BF)
    store_c = pltpu.VMEM((tp,) + shard_c.shape, BF)
    sems = pltpu.SemaphoreType.DMA((tp, 8))

    if fast:
        normed, pieces = call(
            functools.partial(project, dims),
            [((tp, block, width), BF), ((seqs, 3, HEAD, queries), BF)],
            me_ref,
            *blocks,
            row_gain,
            row_weight,
            specs=[SMEM] + [VMEM] * (tp + 2),
            flops=2 * cols * width * 3 * features,
            moved=8 << 20,
        )
    else:
        order = jnp.stack(blocks)[my_z ^ jnp.arange(tp)]
        order = order.reshape(tp, slots, ranks, few, width).transpose(0, 2, 1, 3, 4)
        normed = layer_norm(order.astype(F32), row_gain).astype(BF).reshape(tp, block, width)
        pieces = jnp.einsum("fd,zld->fzl", row_weight, normed, preferred_element_type=F32)
        pieces = pieces.astype(BF).reshape(3, heads, HEAD, tp, ranks, part)
        pieces = pieces.transpose(1, 4, 0, 2, 3, 5).reshape(heads, ranks, 3, HEAD, queries)
        pieces = jnp.pad(pieces, ((0, slots - heads),) + ((0, 0),) * 4)
        pieces = pieces.reshape(seqs, 3, HEAD, queries)
    pieces = exchange(pieces, SEQ)
    mixed_shape = (tp * slots, few, seqs * HEAD)
    if fast:
        others = swap(pieces, "r", ranks, 1)
        (mixed,) = call(
            functools.partial(attend, tied_scale),
            [(mixed_shape, BF)],
            pieces,
            others,
            key_ok,
            flops=4 * cols * queries * seqs * HEAD,
            moved=8 << 20,
        )
    else:
        pairs = lax.all_gather(pieces[:, 1:], "r", axis=0)
        pairs = pairs.transpose(2, 1, 3, 0, 4).reshape(2, seqs * HEAD, cols)
        key, value = pairs[0], pairs[1]
        query = pieces[:, 0].reshape(seqs * HEAD, queries)
        key_ok = valid.reshape(1, cols)
        logits = jnp.einsum("ki,kj->ij", query, key, preferred_element_type=F32) * tied_scale
        masked = jnp.where(key_ok > 0, logits, NEGATIVE)
        powers = jnp.exp(masked - jnp.max(masked, axis=-1, keepdims=True))
        probs = powers / jnp.sum(powers, axis=-1, keepdims=True)
        mixed = jnp.einsum("ij,kj->ik", probs.astype(BF), value, preferred_element_type=F32)
        mixed = mixed.astype(BF).reshape(mixed_shape)
    mixed = exchange(mixed, ("tp", "c"))
    attended = (
        mixed.reshape(tp, slots, few, seqs, HEAD)[:, :heads]
        .transpose(0, 3, 2, 1, 4)
        .reshape(tp, count, features)
    )

    flat = (count, width)
    shards = (tp, count, features)
    n_parts = len(parts_a)
    after_row, col_normed, col_proj, col_mixed, after_col = call(
        functools.partial(columns_forward, (few, tp, heads), n_parts),
        [(flat, F32), (flat, BF), ((3,) + shards, BF), (shards, BF), (flat, F32)],
        me_ref,
        residual,
        attended,
        col_gain,
        shard_a,
        *parts_a,
        specs=[SMEM] + [VMEM] * 3 + [ANY] * (1 + n_parts),
        scratch=[store_a, sems],
        flops=2 * count * width * width * 5,
        moved=20 << 20,
    )
    if fast:
        grad_kinds = [((4, tp, width // seqs, hidden), BF)] * 4
        small_kinds = [((4, tp, width // seqs, 5 * features), BF)] * 2
        orders = ((0, 2, 1), (0, 1, 2))
    else:
        grad_kinds = [((tp, width, hidden), BF)] * 2
        small_kinds = [((tp, width, 5 * features), BF)]
        orders = (None, None)
    turned_rows = pltpu.VMEM((width, count), BF)
    outputs, middle, ffn_gain_grad, *wide_grads = call(
        functools.partial(feed_forward, tp, n_parts, orders),
        [(flat, BF), (flat, F32), ((1, width), F32)] + grad_kinds,
        me_ref,
        after_col,
        given,
        ffn_gain,
        up_own,
        down_own,
        *parts_b,
        specs=[SMEM] + [VMEM] * 3 + [ANY] * (2 + n_parts),
        scratch=[turned_rows, store_b, sems],
        flops=2 * count * width * hidden * tp * 6,
        moved=30 << 20,
    )
    outputs = exchange(outputs.reshape(seqs, few, width), SEQ).reshape(block, width)
    inner, inner_low, row_mixed, col_gain_grad, *small_grads = call(
        functools.partial(columns_backward, (few, tp, heads), n_parts, orders[1]),
        [(flat, F32), (flat, BF), (shards, BF), ((1, width), F32)] + small_kinds,
        me_ref,
        middle,
        after_row,
        col_normed,
        col_proj,
        col_mixed,
        attended,
        col_gain,
        shard_a,
        *parts_a,
        specs=[SMEM] + [VMEM] * 7 + [ANY] * (1 + n_parts),
        scratch=[pltpu.VMEM((3, count, features), BF), turned_rows, store_a, sems],
        flops=2 * count * width * width * 10,
        moved=30 << 20,
    )

    def first(kept, sent):
        return add(kept, swap(sent, "r", ranks, 1))

    def second(held, mask):
        half = held.shape[0] // 2
        return add(held[:half], swap(held[half:], "c", slots, mask))

    def last(held):
        total = held[0].astype(F32)
        for k in range(1, tp):
            total = total + swap(held[k], "tp", tp, k).astype(F32)
        return total

    def all_at_once(grad):
        grad = lax.psum_scatter(grad, SEQ, scatter_dimension=1, tiled=True)
        return lax.psum_scatter(grad, "tp", scatter_dimension=0, tiled=True)[0].astype(F32)

    row_mixed = row_mixed.reshape(tp, seqs, few, heads, HEAD).transpose(0, 3, 2, 1, 4)
    row_mixed = jnp.pad(row_mixed, ((0, 0), (0, slots - heads)) + ((0, 0),) * 3)
    row_mixed = exchange(row_mixed.reshape(mixed_shape), ("tp", "c"))
    inner_home = exchange(inner_low.reshape(seqs, few, width), SEQ).reshape(block, width)
    if fast:
        up_sum, down_sum = first(*wide_grads[:2]), first(*wide_grads[2:])
        row_mixed = after(row_mixed, up_sum, down_sum)
        query_grad, kept, sent = call(
            functools.partial(attend_back, tied_scale),
            [
                ((seqs, HEAD, queries), BF),
                ((seqs, 2, HEAD, queries), F32),
                ((seqs, 2, HEAD, queries), BF),
            ],
            pieces,
            others,
            key_ok,
            query_weight,
            row_mixed,
            flops=10 * cols * queries * seqs * HEAD,
            moved=16 << 20,
        )
        pair_grad = (kept + swap(sent, "r", ranks, 1).astype(F32)).astype(BF)
    else:
        out_grad = row_mixed.reshape(queries, seqs * HEAD)
        prob_grad = jnp.einsum("ik,kj->ij", out_grad, value, preferred_element_type=F32)
        prob_dot = jnp.sum(probs * prob_grad, axis=-1, keepdims=True)
        mean_logit = jnp.sum(
            jnp.where(key_ok > 0, probs * masked, 0.0), axis=-1, keepdims=True
        )
        entropy = jnp.where(key_ok > 0, probs * (masked - mean_logit), 0.0)
        grad = (probs * (prob_grad - prob_dot) - query_weight * entropy).astype(BF)
        total = jnp.einsum("ij,kj->ki", grad, key, preferred_element_type=F32)
        query_grad = (total * tied_scale).astype(BF).reshape(seqs, HEAD, queries)
        key_grad = jnp.einsum("ki,ij->kj", query, grad, preferred_element_type=F32)
        value_grad = jnp.einsum(
            "ik,ij->kj", out_grad, probs.astype(BF), preferred_element_type=F32
        )
        both = jnp.stack([(key_grad * tied_scale).astype(BF), value_grad.astype(BF)])
        both = both.reshape(2, seqs, HEAD, ranks, queries).transpose(3, 1, 0, 2, 4)
        pair_grad = lax.psum_scatter(both, "r", scatter_dimension=0, tiled=False)
    row_grad = exchange(jnp.concatenate([query_grad[:, None], pair_grad], axis=1), SEQ)
    if fast:
        up_sum, down_sum = second(up_sum, 2), second(down_sum, 1)
        small_sum = first(*small_grads)
        row_grad = after(row_grad, up_sum, down_sum, small_sum)
        *pieces, kept, sent, row_gain_grad = call(
            functools.partial(gather_grads, dims, (0, 2, 1)),
            [((3 * features, block), BF)] * tp
            + [((4, width // seqs, 3 * features), BF)] * 2
            + [((1, width), F32)],
            me_ref,
            row_grad,
            normed,
            row_gain,
            row_weight,
            specs=[SMEM] + [VMEM] * 4,
            scratch=[pltpu.VMEM((width, 3 * features), BF)],
            flops=2 * cols * width * 3 * features,
            moved=8 << 20,
        )
    else:
        both = row_grad.reshape(slots, ranks, 3, HEAD, tp, part)[:heads]
        both = both.transpose(4, 2, 0, 3, 1, 5).reshape(tp, 3 * features, block)
        row_grad = jnp.einsum("zld,zfl->df", normed, both, preferred_element_type=F32)
        row_gain_grad = (
            jnp.sum(row_grad.T * row_weight.astype(F32), axis=0, keepdims=True) / row_gain
        )
        pieces = [both[my_z ^ k] for k in range(tp)]
    pieces = [pieces[0]] + [swap(pieces[k], "tp", tp, k) for k in range(1, tp)]
    gains = jnp.concatenate([row_gain_grad, col_gain_grad, ffn_gain_grad], axis=0)
    for axis, size in (("r", ranks), ("c", slots), ("tp", tp)):
        for k in bits_of(size):
            gains = gains + swap(gains, axis, size, k)
    if fast:
        up_sum, down_sum = second(up_sum, 1)[0], second(down_sum, 2)[0]
        small_sum = second(small_sum, 1)
        row_grad = first(kept, sent)
        pieces[1] = after(pieces[1], up_sum, down_sum, small_sum, row_grad)
    (input_grad,) = call(
        functools.partial(finish, dims, n_parts),
        [((block, width), BF)],
        me_ref,
        *pieces,
        own,
        row_gain,
        inner_home,
        shard_c,
        *parts_c,
        specs=[SMEM] + [VMEM] * (tp + 3) + [ANY] * (1 + n_parts),
        scratch=[store_c, sems],
        flops=2 * block * width * width * 3,
        moved=8 << 20,
    )
    if fast:
        small_sum = second(small_sum, 2)[0]
        row_grad = second(row_grad, 2)
        row_grad = second(row_grad, 1)[0].astype(F32)
        up_grad, down_grad, small = last(up_sum), last(down_sum), last(small_sum)
    else:
        row_grad = lax.psum_scatter(row_grad, SEQ, scatter_dimension=0, tiled=True)
        up_grad, down_grad = all_at_once(wide_grads[0]), all_at_once(wide_grads[1])
        small = all_at_once(small_grads[0])

    def thirds(value):
        return value.reshape(width // seqs, 3, features).transpose(1, 0, 2)

    return (
        outputs[None, None],
        input_grad[None, None],
        gains[0],
        thirds(row_grad),
        small[:, 4 * features :].T,
        gains[1],
        thirds(small[:, : 3 * features]),
        small[:, 3 * features : 4 * features].T,
        gains[2],
        up_grad,
        down_grad.T,
    )


def solution(mesh):
    seqs, tp = mesh.shape["seq"], mesh.shape["tp"]
    heads = HEADS // tp
    slots = 1 << (heads - 1).bit_length()
    split = Mesh(mesh.devices.reshape(slots, seqs // slots, tp), ("c", "r", "tp"))
    return jax.shard_map(
        local,
        mesh=split,
        in_specs=(
            P(None, SEQ, "tp", None),
            P(None, SEQ, "tp", None),
            P(),
            P(),
            P(),
            P(None, None, "tp"),
            P("tp", None),
            P(),
            P(None, None, "tp"),
            P("tp", None),
            P(),
            P(None, "tp"),
            P("tp", None),
        ),
        out_specs=(
            P(None, SEQ, "tp", None),
            P(None, SEQ, "tp", None),
            P(),
            P(None, SEQ, "tp"),
            P("tp", SEQ),
            P(),
            P(None, SEQ, "tp"),
            P("tp", SEQ),
            P(),
            P(SEQ, "tp"),
            P("tp", SEQ),
        ),
        check_vma=False,
    )
```

```python
import functools

import jax
import jax.numpy as jnp
from jax import lax
from jax.experimental import pallas as pl
from jax.experimental.pallas import tpu as pltpu
from jax.sharding import Mesh
from jax.sharding import PartitionSpec as P

HEADS = 12
HEAD = 64
EPSILON = 1e-05
NEGATIVE = -1e30
ENTROPY_WEIGHT = 4.0

SEQ = ("c", "r")
BF = jnp.bfloat16
F32 = jnp.float32
VMEM_LIMIT = 60 * 1024 * 1024


def statistics(value):
    average = jnp.mean(value, axis=-1, keepdims=True)
    centred = value - average
    inverse = lax.rsqrt(jnp.mean(centred * centred, axis=-1, keepdims=True) + EPSILON)
    return centred * inverse, inverse


def layer_norm(value, gain):
    unit, _ = statistics(value)
    return unit * gain


def norm_back(value, gain, upstream):
    unit, inverse = statistics(value)
    scaled = upstream * gain
    back = inverse * (
        scaled
        - jnp.mean(scaled, axis=-1, keepdims=True)
        - unit * jnp.mean(scaled * unit, axis=-1, keepdims=True)
    )
    return back, jnp.sum(upstream * unit, axis=0, keepdims=True)


def gelu_parts(value):
    share = 0.5 * (1.0 + lax.erf(value * (0.5**0.5)))
    slope = share + value * jnp.exp(-0.5 * value * value) * 0.3989422804014327
    return value * share, slope


def mm(left, right):
    return lax.dot_general(left, right, (((1,), (0,)), ((), ())), preferred_element_type=F32)


def mm_nt(left, right):
    return lax.dot_general(left, right, (((1,), (1,)), ((), ())), preferred_element_type=F32)


def swap(value, axis, size, mask):
    return lax.ppermute(value, axis, [(i, i ^ mask) for i in range(size)])


def bits_of(size):
    return [1 << b for b in range(size.bit_length() - 1)]


def exchange(value, axis):
    return lax.all_to_all(value, axis, split_axis=0, concat_axis=0, tiled=True)


ANY = pl.BlockSpec(memory_space=pl.ANY)
VMEM = pl.BlockSpec(memory_space=pltpu.VMEM)
SMEM = pl.BlockSpec(memory_space=pltpu.SMEM)


def call(body, outs, *args, specs=None, scratch=(), flops=0, moved=0):
    inner = body.func if isinstance(body, functools.partial) else body
    cost = pl.CostEstimate(flops=int(flops), bytes_accessed=int(moved), transcendentals=0)
    return pl.pallas_call(
        body,
        out_shape=[jax.ShapeDtypeStruct(shape, kind) for shape, kind in outs],
        in_specs=[VMEM] * len(args) if specs is None else specs,
        out_specs=[VMEM] * len(outs),
        scratch_shapes=list(scratch),
        compiler_params=pltpu.CompilerParams(vmem_limit_bytes=VMEM_LIMIT),
        cost_estimate=cost if flops else None,
        name=inner.__name__,
    )(*args)


def shard_copies(me_ref, tp, own, parts, store, sems):
    copies = [own]
    for k in range(1, tp):
        group = []
        if len(parts) == 1:
            source = parts[0].at[me_ref[1] ^ k]
            group.append(pltpu.make_async_copy(source, store.at[k], sems.at[k, 0]))
        else:
            for core, part in enumerate(parts):
                rows = part.shape[1] // 4
                for chip in range(4):
                    source = part.at[k - 1, pl.ds(chip * rows, rows)]
                    target = store.at[k, me_ref[0] ^ (2 * chip + core)]
                    sem = sems.at[k, 2 * chip + core]
                    group.append(pltpu.make_async_copy(source, target, sem))
        copies.append(group)
    for group in copies:
        for copy in group:
            copy.start()

    def wait(k):
        for copy in copies[k]:
            copy.wait()

    return wait


def fetch(me_ref, tp, shard, parts, store, sems):
    own = [pltpu.make_async_copy(shard, store.at[0], sems.at[0, 0])]
    return shard_copies(me_ref, tp, own, parts, store, sems)


def relative_rows(me_ref, order, turned, store, count=None):
    if order is None:
        return turned
    store[...] = turned
    rows = turned.shape[0] >> len(order)
    picked = []
    for m in range(1 << len(order) if count is None else count):
        mask = sum(((m >> (len(order) - 1 - i)) & 1) << bit for i, bit in enumerate(order))
        start = pl.multiple_of((me_ref[0] ^ mask) * rows, rows)
        picked.append(store[pl.ds(start, rows), :])
    return jnp.concatenate(picked, axis=0)


def project(dims, me_ref, blocks, gain, weight, normed, pieces):
    slots, ranks, few, tp, heads = dims
    features = heads * HEAD
    part = slots * few
    pieces[heads * ranks :] = jnp.zeros_like(pieces[heads * ranks :])
    for k in range(tp):
        z = me_ref[1] ^ k
        value = blocks[z].astype(F32).reshape(slots, ranks, few, -1)
        value = jnp.concatenate(
            [value[c, r] for r in range(ranks) for c in range(slots)], axis=0
        )
        low = layer_norm(value, gain[...]).astype(BF)
        normed[z] = low
        columns = pl.ds(pl.multiple_of(z * part, part), part)
        proj = mm_nt(weight[...], low).astype(BF)
        for c in range(heads):
            for r in range(ranks):
                for t in range(3):
                    rows = t * features + c * HEAD
                    piece = proj[rows : rows + HEAD, r * part : (r + 1) * part]
                    pieces[c * ranks + r, t, :, columns] = piece


def tied_softmax(own, other, key_ok, scale):
    depth = own.shape[0] * own.shape[2]
    turned = own[:, 0].reshape(depth, -1).T
    logits = jnp.concatenate(
        [mm(turned, pair[:, 1].reshape(depth, -1)) for pair in (own, other)], axis=1
    )
    ok = key_ok[...] > 0
    masked = jnp.where(ok, logits * scale, NEGATIVE)
    powers = jnp.exp(masked - jnp.max(masked, axis=-1, keepdims=True))
    return masked, powers * (1.0 / jnp.sum(powers, axis=-1, keepdims=True)), ok


def attend(scale, own, other, key_ok, mixed):
    _, probs, _ = tied_softmax(own, other, key_ok, scale)
    depth = own.shape[0] * own.shape[2]
    low = probs.astype(BF)
    half = low.shape[1] // 2
    total = mm_nt(low[:, :half], own[:, 2].reshape(depth, -1))
    total += mm_nt(low[:, half:], other[:, 2].reshape(depth, -1))
    mixed[...] = total.astype(BF).reshape(mixed.shape)


def attend_back(scale, own, other, key_ok, weight, mixed_grad, query_grad, kept, given):
    masked, probs, ok = tied_softmax(own, other, key_ok, scale)
    seqs = own.shape[0]
    depth = seqs * own.shape[2]
    low = probs.astype(BF)
    half = low.shape[1] // 2
    out_grad = mixed_grad[...].reshape(-1, depth)
    prob_grad = jnp.concatenate(
        [mm(out_grad, pair[:, 2].reshape(depth, -1)) for pair in (own, other)], axis=1
    )
    prob_dot = jnp.sum(probs * prob_grad, axis=-1, keepdims=True)
    mean_logit = jnp.sum(jnp.where(ok, probs * masked, 0.0), axis=-1, keepdims=True)
    entropy = jnp.where(ok, probs * (masked - mean_logit), 0.0)
    grad = (probs * (prob_grad - prob_dot) - weight[...] * entropy).astype(BF)
    total = mm_nt(own[:, 1].reshape(depth, -1), grad[:, :half])
    total += mm_nt(other[:, 1].reshape(depth, -1), grad[:, half:])
    query_grad[...] = (total * scale).astype(BF).reshape(query_grad.shape)
    turned = out_grad.T
    flat = own[:, 0].reshape(depth, -1)
    shape = (seqs, HEAD, half)
    given[:, 0] = (mm(flat, grad[:, half:]) * scale).astype(BF).reshape(shape)
    given[:, 1] = mm(turned, low[:, half:]).astype(BF).reshape(shape)
    kept[:, 0] = (mm(flat, grad[:, :half]) * scale).reshape(shape)
    kept[:, 1] = mm(turned, low[:, :half]).reshape(shape)


def column_probs(query, key, rule, scale):
    scores = jnp.where(rule, mm_nt(query, key) * scale, NEGATIVE)
    powers = jnp.exp(scores - jnp.max(scores, axis=-1, keepdims=True))
    return powers * (1.0 / jnp.sum(powers, axis=-1, keepdims=True))


def same_column(count, few):
    rows = lax.broadcasted_iota(jnp.int32, (count, count), 0)
    columns = lax.broadcasted_iota(jnp.int32, (count, count), 1)
    return (rows % few) == (columns % few)


def narrow(store, k, features):
    whole = store[k].reshape(-1, store.shape[3])
    return [whole[i * features : (i + 1) * features] for i in range(5)]


def columns_forward(dims, parts, me_ref, both, arrived, gain, shard, *refs):
    few, tp, heads = dims
    parts, refs = refs[:parts], refs[parts:]
    after_row, normed, proj, right, after_col, store, sems = refs
    wait = fetch(me_ref, tp, shard, parts, store, sems)
    features = heads * HEAD
    seqs = both.shape[0]
    count = seqs * few
    total = both[:, 0].reshape(count, -1).astype(F32)
    attended = []
    for k in range(tp):
        z = me_ref[1] ^ k
        if len(arrived.shape) == 4:
            lanes = []
            for c in range(heads):
                value = arrived[z, c]
                pieces = [value[:, s * HEAD : (s + 1) * HEAD] for s in range(seqs)]
                lanes.append(jnp.concatenate(pieces, axis=0))
            attended.append(jnp.concatenate(lanes, axis=1))
        else:
            attended.append(arrived[z])
        right[k, :, 4 * features : 5 * features] = attended[k]
        right[k, :, 5 * features :] = jnp.zeros_like(right[k, :, 5 * features :])
    update = jnp.zeros_like(total)
    for k in range(tp):
        wait(k)
        update += mm(attended[k], narrow(store, k, features)[0])
    total = total + update
    after_row[...] = total
    low = layer_norm(total, gain[...]).astype(BF)
    normed[...] = low
    rule = same_column(count, few)
    update = jnp.zeros_like(total)
    for k in range(tp):
        weights = narrow(store, k, features)
        for t in range(3):
            proj[t, k] = mm_nt(low, weights[2 + t]).astype(BF)
        mixed = []
        for h in range(heads):
            at = slice(h * HEAD, (h + 1) * HEAD)
            probs = column_probs(proj[0, k, :, at], proj[1, k, :, at], rule, HEAD**-0.5)
            mixed.append(mm(probs.astype(BF), proj[2, k, :, at]).astype(BF))
        mixed = jnp.concatenate(mixed, axis=1)
        right[k, :, 3 * features : 4 * features] = mixed
        update += mm(mixed, weights[1])
    after_col[...] = total + update


def columns_backward(dims, parts, me_ref, *refs):
    few, tp, heads = dims
    middle, outputs, after_row, normed, proj, right, gain, shard = refs[:8]
    parts, refs = refs[8 : 8 + parts], refs[8 + parts :]
    home, left, right_out, row_mixed, gain_grad, store, sems = refs
    wait = fetch(me_ref, tp, shard, parts, store, sems)
    features = heads * HEAD
    count = middle.shape[0]
    seqs = count // few
    middle_low = middle[...].astype(BF)
    left[0] = normed[...]
    left[1] = middle_low
    rule = same_column(count, few)
    upstream = jnp.zeros(middle.shape, F32)
    for k in range(tp):
        wait(k)
        weights = narrow(store, k, features)
        mixed_grad = mm_nt(middle_low, weights[1]).astype(BF)
        grads = [[], [], []]
        for h in range(heads):
            at = slice(h * HEAD, (h + 1) * HEAD)
            query, key, value = proj[0, k, :, at], proj[1, k, :, at], proj[2, k, :, at]
            probs = column_probs(query, key, rule, HEAD**-0.5)
            out_grad = mixed_grad[:, at]
            prob_grad = mm_nt(out_grad, value)
            score = probs * (prob_grad - jnp.sum(probs * prob_grad, axis=-1, keepdims=True))
            score = score.astype(BF)
            grads[0].append((mm(score, key) * HEAD**-0.5).astype(BF))
            grads[1].append((mm(score.T, query) * HEAD**-0.5).astype(BF))
            grads[2].append(mm(probs.astype(BF).T, out_grad).astype(BF))
        for t in range(3):
            grad = jnp.concatenate(grads[t], axis=1)
            upstream += mm(grad, weights[2 + t])
            right_out[k, :, t * features : (t + 1) * features] = grad
        right_out[k, :, 3 * features :] = right[k, :, 3 * features :]
    back, gain_grad[...] = norm_back(after_row[...], gain[...], upstream)
    low = (middle[...] + back).astype(BF)
    home[:, 0] = outputs[...].reshape(seqs, few, -1)
    home[:, 1] = low.reshape(seqs, few, -1)
    left[2] = low
    for k in range(tp):
        z = me_ref[1] ^ k
        value = mm_nt(low, narrow(store, k, features)[0]).astype(BF)
        if len(row_mixed.shape) == 4:
            for c in range(heads):
                lane = value[:, c * HEAD : (c + 1) * HEAD]
                pieces = [lane[s * few : (s + 1) * few] for s in range(seqs)]
                row_mixed[z, c] = jnp.concatenate(pieces, axis=1)
            row_mixed[z, heads:] = jnp.zeros_like(row_mixed[z, heads:])
        else:
            row_mixed[z] = value


def store_halves(halves, z, value):
    rows = value.shape[0] // 2
    for half, part in zip(halves, (value[:rows], value[rows:])):
        half[:, z] = part.reshape(half.shape[0], half.shape[2], -1)


def column_weights(orders, me_ref, left, left_other, right, right_other, *refs):
    tp = right.shape[0]
    qkv, col_out, row_out, rows = refs[0:2], refs[2:4], refs[4:6], refs[6]
    features = col_out[0].shape[3]
    turned = []
    for i in range(3):
        value = jnp.concatenate([left[i], left_other[i]], axis=0).T
        turned.append(relative_rows(me_ref, orders[i], value, rows.at[i], 4))
    for k in range(tp):
        value = jnp.concatenate([right[k], right_other[k]], axis=0)
        start = 0
        for i, (halves, size) in enumerate(((qkv, 3), (col_out, 1), (row_out, 1))):
            columns = slice(start, start + size * features)
            store_halves(halves, me_ref[1] ^ k, mm(turned[i], value[:, columns]).astype(BF))
            start += size * features


def wide_weights(orders, me_ref, left, left_other, right, right_other, *refs):
    rows = refs[4]
    for i, grads in enumerate((refs[0:2], refs[2:4])):
        value = jnp.concatenate([left[i], left_other[i]], axis=0).T
        turned = relative_rows(me_ref, orders[i], value, rows.at[i], 4)
        for k in range(right.shape[1]):
            both = jnp.concatenate([right[i, k], right_other[i, k]], axis=0)
            store_halves(grads, me_ref[1] ^ k, mm(turned, both).astype(BF))


def feed_forward(tp, parts, me_ref, after_col, arrived, gain, up_shard, down_shard, *refs):
    parts, refs = refs[:parts], refs[parts:]
    outputs, middle, gain_grad, left, right, store, sems = refs
    half = store.shape[1] // 2
    own = [
        pltpu.make_async_copy(up_shard, store.at[0, pl.ds(0, half)], sems.at[0, 0]),
        pltpu.make_async_copy(down_shard, store.at[0, pl.ds(half, half)], sems.at[0, 1]),
    ]
    wait = shard_copies(me_ref, tp, own, parts, store, sems)
    value = after_col[...]
    low = layer_norm(value, gain[...]).astype(BF)
    given = arrived[:, 1].reshape(value.shape)
    left[0] = low
    left[1] = given
    result = value
    upstream = jnp.zeros_like(value)
    for k in range(tp):
        wait(k)
        up = store[k, :half].reshape(-1, store.shape[3])
        down = store[k, half:].reshape(-1, store.shape[3])
        hidden, slope = gelu_parts(mm(low, up))
        hidden = hidden.astype(BF)
        right[1, k] = hidden
        result += mm(hidden, down)
        pre_grad = (mm_nt(given, down) * slope).astype(BF)
        right[0, k] = pre_grad
        upstream += mm_nt(pre_grad, up)
    outputs[...] = result.astype(BF)
    back, gain_grad[...] = norm_back(value, gain[...], upstream)
    middle[...] = given.astype(F32) + back


def gather_grads(dims, order, me_ref, back, normed, gain, weight, *outs):
    slots, ranks, few, tp, heads = dims
    features = heads * HEAD
    part = slots * few
    pieces, kept, sent, gain_grad, rows = outs
    total = jnp.zeros((3 * features, normed.shape[2]), F32)
    for k in range(tp):
        z = me_ref[1] ^ k
        columns = pl.ds(pl.multiple_of(z * part, part), part)
        for c in range(heads):
            for r in range(ranks):
                for t in range(3):
                    piece = back[c * ranks + r, t, :, columns]
                    at = t * features + c * HEAD
                    pieces[z, at : at + HEAD, r * part : (r + 1) * part] = piece
        total += mm(pieces[z], normed[z])
    gain_grad[...] = (
        jnp.sum(total * weight[...].astype(F32), axis=0, keepdims=True) / gain[...]
    )
    turned = relative_rows(me_ref, order, total.T.astype(BF), rows)
    half = turned.shape[0] // 2
    kept[...] = turned[:half].reshape(kept.shape)
    sent[...] = turned[half:].reshape(sent.shape)


def finish(dims, parts, me_ref, *refs):
    slots, ranks, few, tp, heads = dims
    features = heads * HEAD
    pieces, tokens, gain, home, shard = refs[:5]
    parts, (result, store, sems) = refs[5 : 5 + parts], refs[5 + parts :]
    wait = fetch(me_ref, tp, shard, parts, store, sems)
    inner = home[:, 1].reshape(tokens.shape)
    upstream = jnp.zeros(inner.shape, F32)
    for k in range(tp):
        wait(k)
        whole = store[k].reshape(-1, store.shape[3])[: 3 * features]
        upstream += mm(pieces[me_ref[1] ^ k].T, whole)
    upstream = upstream.reshape(ranks, slots, few, -1)
    upstream = jnp.concatenate(
        [upstream[r, c] for c in range(slots) for r in range(ranks)], axis=0
    )
    back, _ = norm_back(tokens[...].astype(F32), gain[...], upstream)
    result[...] = (inner.astype(F32) + back).astype(BF)


def after(value, *others):
    return lax.optimization_barrier((value,) + others)[0]


def add(left, right):
    return (left.astype(F32) + right.astype(F32)).astype(BF)


def local(
    tokens,
    cotangent,
    lengths,
    column_mask,
    row_gain,
    row_qkv,
    row_out,
    col_gain,
    col_qkv,
    col_out,
    ffn_gain,
    ffn_up,
    ffn_down,
):
    slots, ranks, tp = lax.axis_size("c"), lax.axis_size("r"), lax.axis_size("tp")
    seqs = slots * ranks
    block, width = tokens.shape[2], tokens.shape[3]
    cols = column_mask.shape[1]
    few = block // seqs
    part = slots * few
    features = row_qkv.shape[2]
    heads = features // HEAD
    hidden = ffn_up.shape[1]
    queries = tp * part
    count = seqs * few
    tied_scale = (HEAD * seqs) ** (-0.5)
    my_seq, my_rank, my_z = lax.axis_index(SEQ), lax.axis_index("r"), lax.axis_index("tp")
    me_ref = jnp.stack([my_seq, my_z]).astype(jnp.int32)
    dims = (slots, ranks, few, tp, heads)
    fast = seqs == 8 and ranks == 2
    row_gain, col_gain, ffn_gain = row_gain[None], col_gain[None], ffn_gain[None]

    penalty_scale = ENTROPY_WEIGHT * (seqs * cols) / (HEADS * jnp.sum(lengths).astype(F32))
    position = jnp.arange(cols, dtype=jnp.int32).reshape(tp, slots, ranks, few)
    position = position.transpose(2, 0, 1, 3)
    flag = column_mask.reshape(tp, slots, ranks, few).transpose(2, 0, 1, 3)
    valid = (position < lengths[0]) & ((flag == 1) | (position == 0))
    valid = valid.astype(F32).reshape(ranks, queries)
    key_ok = jnp.concatenate(
        [lax.dynamic_index_in_dim(valid, my_rank ^ k, 0) for k in range(ranks)], axis=1
    )
    query_position = lax.dynamic_index_in_dim(position.reshape(ranks, queries), my_rank, 0)
    query_weight = jnp.where(query_position < lengths[0], penalty_scale, 0.0).reshape(queries, 1)

    own = tokens[0, 0]
    both = [value.reshape(seqs, few, width) for value in (own, cotangent[0, 0])]
    both = exchange(jnp.stack(both, axis=1), SEQ)

    row_weight = row_qkv.transpose(0, 2, 1).reshape(3 * features, width)
    shard_a = jnp.concatenate(
        [row_out, col_out, col_qkv.transpose(0, 2, 1).reshape(3 * features, width)]
    )

    def cut(shard, least):
        rows = shard.shape[0]
        rows += -rows % (seqs * least)
        shard = jnp.pad(shard, ((0, rows - shard.shape[0]), (0, 0)))
        return shard.reshape(seqs, rows // seqs, width)

    shard_a = cut(shard_a, 16 if fast else 1)
    shard_c = cut(row_weight, 16 if fast else 1)
    shard_b = cut(jnp.concatenate([ffn_up, ffn_down]), 1)

    def mine(shard):
        return lax.dynamic_index_in_dim(shard, my_seq, 0, keepdims=False)

    def everyone(value):
        return exchange(jnp.broadcast_to(value, (tp,) + value.shape), "tp")

    def along_tp(piece):
        return jnp.stack([swap(piece, "tp", tp, k) for k in range(1, tp)])

    def along_plane(held):
        return [swap(held, "c", slots, mask) for mask in (1, 2)]

    def across_plane(near):
        half = near[0].shape[1] // 2
        one = swap(near[0][:, :half], "c", slots, 2)
        return [one, swap(near[1][:, half:], "c", slots, 1)]

    def along_cores(parts):
        held = jnp.concatenate(parts, axis=1)
        return [held, swap(held, "r", ranks, 1)]

    if fast:
        near_a = along_tp(mine(shard_a))
        blocks = everyone(after(own, near_a, both))
        plane_a = along_plane(near_a)
        cross_a = across_plane(plane_a)
        parts_a = along_cores([near_a] + plane_a + cross_a)
        near_b = along_tp(after(mine(shard_b), blocks))
        blocks = after(blocks, *cross_a)
    else:
        blocks = everyone(own)

        def everywhere(shard):
            rows = shard.shape[0] * shard.shape[1]
            whole = lax.all_gather(mine(shard), ("tp",) + SEQ, axis=0)
            return [whole.reshape(tp, 8, rows // 8, width)]

        parts_a, parts_b, parts_c = everywhere(shard_a), everywhere(shard_b), everywhere(shard_c)
        shard_a = shard_a.reshape(8, -1, width)
        shard_c = shard_c.reshape(8, -1, width)
    up_own = ffn_up.reshape(4, -1, width)
    down_own = ffn_down.reshape(4, -1, width)
    store_a = pltpu.VMEM((tp,) + shard_a.shape, BF)
    store_b = pltpu.VMEM((tp, 8, shard_b.shape[0] * shard_b.shape[1] // 8, width), BF)
    store_c = pltpu.VMEM((tp,) + shard_c.shape, BF)
    sems = pltpu.SemaphoreType.DMA((tp, 10))

    if fast:
        normed, pieces = call(
            functools.partial(project, dims),
            [((tp, block, width), BF), ((seqs, 3, HEAD, queries), BF)],
            me_ref,
            blocks,
            row_gain,
            row_weight,
            specs=[SMEM] + [VMEM] * 3,
            flops=2 * cols * width * 3 * features,
            moved=8 << 20,
        )
    else:
        order = blocks.reshape(tp, slots, ranks, few, width).transpose(0, 2, 1, 3, 4)
        normed = layer_norm(order.astype(F32), row_gain).astype(BF).reshape(tp, block, width)
        pieces = jnp.einsum("fd,zld->fzl", row_weight, normed, preferred_element_type=F32)
        pieces = pieces.astype(BF).reshape(3, heads, HEAD, tp, ranks, part)
        pieces = pieces.transpose(1, 4, 0, 2, 3, 5).reshape(heads, ranks, 3, HEAD, queries)
        pieces = jnp.pad(pieces, ((0, slots - heads),) + ((0, 0),) * 4)
        pieces = pieces.reshape(seqs, 3, HEAD, queries)
    pieces = exchange(pieces, SEQ)
    mixed_shape = (tp * slots, few, seqs * HEAD)
    if fast:
        pieces, near_b, *parts_a = lax.optimization_barrier((pieces, near_b, *parts_a))
        others = swap(pieces, "r", ranks, 1)
        plane_b = along_plane(near_b)
        (mixed,) = call(
            functools.partial(attend, tied_scale),
            [(mixed_shape, BF)],
            pieces,
            others,
            key_ok,
            flops=4 * cols * queries * seqs * HEAD,
            moved=8 << 20,
        )
    else:
        pairs = lax.all_gather(pieces[:, 1:], "r", axis=0)
        pairs = pairs.transpose(2, 1, 3, 0, 4).reshape(2, seqs * HEAD, cols)
        key, value = pairs[0], pairs[1]
        query = pieces[:, 0].reshape(seqs * HEAD, queries)
        key_ok = valid.reshape(1, cols)
        logits = jnp.einsum("ki,kj->ij", query, key, preferred_element_type=F32) * tied_scale
        masked = jnp.where(key_ok > 0, logits, NEGATIVE)
        powers = jnp.exp(masked - jnp.max(masked, axis=-1, keepdims=True))
        probs = powers / jnp.sum(powers, axis=-1, keepdims=True)
        mixed = jnp.einsum("ij,kj->ik", probs.astype(BF), value, preferred_element_type=F32)
        mixed = mixed.astype(BF).reshape(mixed_shape)
    mixed = exchange(mixed, ("tp", "c"))
    shards = (tp, count, features)
    if fast:
        arrived = after(mixed, *plane_b).reshape(tp, slots, few, seqs * HEAD)
        parts_b = along_cores([near_b] + plane_b + across_plane(plane_b))
        near_c = along_tp(after(mine(shard_c), mixed))
    else:
        arrived = (
            mixed.reshape(tp, slots, few, seqs, HEAD)[:, :heads]
            .transpose(0, 3, 2, 1, 4)
            .reshape(shards)
        )

    flat = (count, width)
    packed = (tp, count, 5 * features + -5 * features % 128)
    n_parts = len(parts_a)
    after_row, col_normed, col_proj, col_right, after_col = call(
        functools.partial(columns_forward, (few, tp, heads), n_parts),
        [(flat, F32), (flat, BF), ((3,) + shards, BF), (packed, BF), (flat, F32)],
        me_ref,
        both,
        arrived,
        col_gain,
        shard_a,
        *parts_a,
        specs=[SMEM] + [VMEM] * 3 + [ANY] * (1 + n_parts),
        scratch=[store_a, sems],
        flops=2 * count * width * width * 5,
        moved=20 << 20,
    )
    if fast:
        after_col = after(after_col, near_c)
    outputs, middle, ffn_gain_grad, wide_left, wide_right = call(
        functools.partial(feed_forward, tp, n_parts),
        [
            (flat, BF),
            (flat, F32),
            ((1, width), F32),
            ((2,) + flat, BF),
            ((2, tp, count, hidden), BF),
        ],
        me_ref,
        after_col,
        both,
        ffn_gain,
        up_own,
        down_own,
        *parts_b,
        specs=[SMEM] + [VMEM] * 3 + [ANY] * (2 + n_parts),
        scratch=[store_b, sems],
        flops=2 * count * width * hidden * tp * 4,
        moved=30 << 20,
    )
    home, col_left, col_right, row_mixed, col_gain_grad = call(
        functools.partial(columns_backward, (few, tp, heads), n_parts),
        [
            ((seqs, 2, few, width), BF),
            ((3,) + flat, BF),
            (packed, BF),
            ((tp, slots, few, seqs * HEAD) if fast else shards, BF),
            ((1, width), F32),
        ],
        me_ref,
        middle,
        outputs,
        after_row,
        col_normed,
        col_proj,
        col_right,
        col_gain,
        shard_a,
        *parts_a,
        specs=[SMEM] + [VMEM] * 7 + [ANY] * (1 + n_parts),
        scratch=[store_a, sems],
        flops=2 * count * width * width * 8,
        moved=30 << 20,
    )

    def halve(kept, came):
        half = kept.shape[0] // 2
        return add(kept[:half], came[:half]), add(kept[half:], came[half:])

    def give(sent, mask):
        return swap(sent, "c", slots, mask)

    def last(held):
        return jnp.sum(exchange(held, "tp").astype(F32), axis=0)

    def all_at_once(left, right):
        grad = jnp.einsum("ld,zlf->zdf", left, right, preferred_element_type=F32).astype(BF)
        grad = lax.psum_scatter(grad, SEQ, scatter_dimension=1, tiled=True)
        return lax.psum_scatter(grad, "tp", scatter_dimension=0, tiled=True)[0].astype(F32)

    rows_of = width // seqs
    turned_rows = pltpu.VMEM((3, width, 2 * count), BF)
    if fast:
        wide_others = swap(wide_left, "r", ranks, 1), swap(wide_right, "r", ranks, 1)
        col_others = swap(col_left, "r", ranks, 1), swap(col_right, "r", ranks, 1)
        up_kept, up_sent, down_kept, down_sent = call(
            functools.partial(wide_weights, ((0, 2, 1), (0, 1, 2))),
            [((2, tp, rows_of, hidden), BF)] * 4,
            me_ref,
            wide_left,
            wide_others[0],
            wide_right,
            wide_others[1],
            specs=[SMEM] + [VMEM] * 4,
            scratch=[turned_rows],
            flops=2 * count * width * hidden * tp * 2,
            moved=30 << 20,
        )
        qkv_kept, qkv_sent, *outs_halves = call(
            functools.partial(column_weights, ((0, 2, 1), (0, 1, 2), (0, 1, 2))),
            [((2, tp, rows_of, 3 * features), BF)] * 2
            + [((2, tp, rows_of, features), BF)] * 4,
            me_ref,
            after(col_left, up_sent),
            col_others[0],
            col_right,
            col_others[1],
            specs=[SMEM] + [VMEM] * 4,
            scratch=[turned_rows],
            flops=2 * count * width * width * 5,
            moved=12 << 20,
        )
    else:
        row_mixed = row_mixed.reshape(tp, seqs, few, heads, HEAD).transpose(0, 3, 2, 1, 4)
        row_mixed = jnp.pad(row_mixed, ((0, 0), (0, slots - heads)) + ((0, 0),) * 3)
        my_order = my_z ^ jnp.arange(tp)
        col_right = col_right[my_order]
    row_mixed = exchange(row_mixed.reshape(mixed_shape), ("tp", "c"))
    if fast:
        up_came, down_came = give(up_sent, 2), give(down_sent, 1)
        row_mixed = after(row_mixed, qkv_sent)
        query_grad, kept, sent = call(
            functools.partial(attend_back, tied_scale),
            [
                ((seqs, HEAD, queries), BF),
                ((seqs, 2, HEAD, queries), F32),
                ((seqs, 2, HEAD, queries), BF),
            ],
            pieces,
            others,
            key_ok,
            query_weight,
            row_mixed,
            flops=10 * cols * queries * seqs * HEAD,
            moved=16 << 20,
        )
        sent = after(sent, up_came, down_came)
        pair_grad = (kept + swap(sent, "r", ranks, 1).astype(F32)).astype(BF)
        back = jnp.concatenate([query_grad[:, None], pair_grad], axis=1)
    else:
        out_grad = row_mixed.reshape(queries, seqs * HEAD)
        prob_grad = jnp.einsum("ik,kj->ij", out_grad, value, preferred_element_type=F32)
        prob_dot = jnp.sum(probs * prob_grad, axis=-1, keepdims=True)
        mean_logit = jnp.sum(
            jnp.where(key_ok > 0, probs * masked, 0.0), axis=-1, keepdims=True
        )
        entropy = jnp.where(key_ok > 0, probs * (masked - mean_logit), 0.0)
        grad = (probs * (prob_grad - prob_dot) - query_weight * entropy).astype(BF)
        total = jnp.einsum("ij,kj->ki", grad, key, preferred_element_type=F32)
        query_grad = (total * tied_scale).astype(BF).reshape(seqs, HEAD, queries)
        key_grad = jnp.einsum("ki,ij->kj", query, grad, preferred_element_type=F32)
        value_grad = jnp.einsum(
            "ik,ij->kj", out_grad, probs.astype(BF), preferred_element_type=F32
        )
        both = jnp.stack([(key_grad * tied_scale).astype(BF), value_grad.astype(BF)])
        both = both.reshape(2, seqs, HEAD, ranks, queries).transpose(3, 1, 0, 2, 4)
        pair_grad = lax.psum_scatter(both, "r", scatter_dimension=0, tiled=False)
        back = jnp.concatenate([query_grad[:, None], pair_grad], axis=1)
    back = exchange(back, SEQ)
    if fast:
        home = after(home, back)
    home = exchange(home, SEQ)
    outputs = home[:, 0].reshape(block, width)
    if fast:
        (up_kept, up_sent), (down_kept, down_sent) = halve(up_kept, up_came), halve(down_kept, down_came)
        up_came, down_came = give(up_sent, 1), give(down_sent, 2)
        wide_last = jnp.concatenate(
            [add(up_kept, up_came)[0], add(down_kept, down_came)[0]], axis=-1
        )
        col_out_kept, col_out_sent, row_out_kept, row_out_sent = outs_halves
        outs_kept = jnp.concatenate([col_out_kept, row_out_kept], axis=3)
        outs_sent = jnp.concatenate([col_out_sent, row_out_sent], axis=3)
        near_c, qkv_sent, outs_sent, back = lax.optimization_barrier(
            (near_c, qkv_sent, outs_sent, after(back, up_came, down_came))
        )
        qkv_came, outs_came = give(qkv_sent, 2), give(outs_sent, 1)
        plane_c = along_plane(near_c)
        parts_c = along_cores([near_c] + plane_c + across_plane(plane_c))
        traded, kept, sent, row_gain_grad = call(
            functools.partial(gather_grads, dims, (0, 2, 1)),
            [((tp, 3 * features, block), BF)]
            + [((4, rows_of, 3 * features), BF)] * 2
            + [((1, width), F32)],
            me_ref,
            back,
            normed,
            row_gain,
            row_weight,
            specs=[SMEM] + [VMEM] * 4,
            scratch=[pltpu.VMEM((width, 3 * features), BF)],
            flops=2 * cols * width * 3 * features,
            moved=8 << 20,
        )
    else:
        both = back.reshape(slots, ranks, 3, HEAD, tp, part)[:heads]
        both = both.transpose(4, 2, 0, 3, 1, 5).reshape(tp, 3 * features, block)
        row_grad = jnp.einsum("zld,zfl->df", normed, both, preferred_element_type=F32)
        row_gain_grad = (
            jnp.sum(row_grad.T * row_weight.astype(F32), axis=0, keepdims=True) / row_gain
        )
        traded = both
    traded = exchange(traded, "tp")
    if fast:
        row_gain_grad = after(row_gain_grad, traded)
    gains = jnp.concatenate([row_gain_grad, col_gain_grad, ffn_gain_grad], axis=0)
    for axis, size in (("r", ranks), ("c", slots), ("tp", tp)):
        for k in bits_of(size):
            gains = gains + swap(gains, axis, size, k)
    if fast:
        came = swap(sent, "r", ranks, 1)
        kept, sent = add(kept[:2], came[:2]), add(kept[2:], came[2:])
        kept, sent = halve(kept, give(sent, 2))
        row_grad = add(kept[0], give(sent, 1)[0]).astype(F32)
        (qkv_kept, qkv_sent), (outs_kept, outs_sent) = halve(qkv_kept, qkv_came), halve(outs_kept, outs_came)
        small = jnp.concatenate(
            [add(qkv_kept, give(qkv_sent, 1))[0], add(outs_kept, give(outs_sent, 2))[0]], axis=-1
        )
        wide_grad = last(after(wide_last, traded))
        small = last(small)
        qkv, outs = small[:, : 3 * features], small[:, 3 * features :]
        up_grad, down_grad = wide_grad[:, :hidden], wide_grad[:, hidden:]
    (input_grad,) = call(
        functools.partial(finish, dims, n_parts),
        [((block, width), BF)],
        me_ref,
        traded,
        own,
        row_gain,
        home,
        shard_c,
        *parts_c,
        specs=[SMEM] + [VMEM] * 4 + [ANY] * (1 + n_parts),
        scratch=[store_c, sems],
        flops=2 * block * width * width * 3,
        moved=8 << 20,
    )
    if not fast:
        row_grad = lax.psum_scatter(row_grad, SEQ, scatter_dimension=0, tiled=True)
        wide_right = wide_right[:, my_order]
        up_grad = all_at_once(wide_left[0], wide_right[0])
        down_grad = all_at_once(wide_left[1], wide_right[1])
        qkv = all_at_once(col_left[0], col_right[..., : 3 * features])
        outs = jnp.concatenate(
            [
                all_at_once(col_left[1], col_right[..., 3 * features : 4 * features]),
                all_at_once(col_left[2], col_right[..., 4 * features : 5 * features]),
            ],
            axis=1,
        )

    def thirds(value):
        return value.reshape(width // seqs, 3, features).transpose(1, 0, 2)

    return (
        outputs[None, None],
        input_grad[None, None],
        gains[0],
        thirds(row_grad),
        outs[:, features:].T,
        gains[1],
        thirds(qkv),
        outs[:, :features].T,
        gains[2],
        up_grad,
        down_grad.T,
    )


def solution(mesh):
    seqs, tp = mesh.shape["seq"], mesh.shape["tp"]
    heads = HEADS // tp
    slots = 1 << (heads - 1).bit_length()
    split = Mesh(mesh.devices.reshape(slots, seqs // slots, tp), ("c", "r", "tp"))
    return jax.shard_map(
        local,
        mesh=split,
        in_specs=(
            P(None, SEQ, "tp", None),
            P(None, SEQ, "tp", None),
            P(),
            P(),
            P(),
            P(None, None, "tp"),
            P("tp", None),
            P(),
            P(None, None, "tp"),
            P("tp", None),
            P(),
            P(None, "tp"),
            P("tp", None),
        ),
        out_specs=(
            P(None, SEQ, "tp", None),
            P(None, SEQ, "tp", None),
            P(),
            P(None, SEQ, "tp"),
            P("tp", SEQ),
            P(),
            P(None, SEQ, "tp"),
            P("tp", SEQ),
            P(),
            P(SEQ, "tp"),
            P("tp", SEQ),
        ),
        check_vma=False,
    )
```

```python
import functools

import jax
import jax.numpy as jnp
from jax import lax
from jax.experimental import pallas as pl
from jax.experimental.pallas import tpu as pltpu
from jax.sharding import Mesh
from jax.sharding import PartitionSpec as P

HEADS = 12
HEAD = 64
EPSILON = 1e-05
NEGATIVE = -1e30
ENTROPY_WEIGHT = 4.0

SEQ = ("c", "r")
BF = jnp.bfloat16
F32 = jnp.float32
VMEM_LIMIT = 60 * 1024 * 1024


def statistics(value):
    average = jnp.mean(value, axis=-1, keepdims=True)
    centred = value - average
    inverse = lax.rsqrt(jnp.mean(centred * centred, axis=-1, keepdims=True) + EPSILON)
    return centred * inverse, inverse


def layer_norm(value, gain):
    unit, _ = statistics(value)
    return unit * gain


def norm_back(value, gain, upstream):
    unit, inverse = statistics(value)
    scaled = upstream * gain
    back = inverse * (
        scaled
        - jnp.mean(scaled, axis=-1, keepdims=True)
        - unit * jnp.mean(scaled * unit, axis=-1, keepdims=True)
    )
    return back, jnp.sum(upstream * unit, axis=0, keepdims=True)


def gelu_parts(value):
    share = 0.5 * (1.0 + lax.erf(value * (0.5**0.5)))
    slope = share + value * jnp.exp(-0.5 * value * value) * 0.3989422804014327
    return value * share, slope


def mm(left, right):
    return lax.dot_general(left, right, (((1,), (0,)), ((), ())), preferred_element_type=F32)


def mm_nt(left, right):
    return lax.dot_general(left, right, (((1,), (1,)), ((), ())), preferred_element_type=F32)


def swap(value, axis, size, mask):
    return lax.ppermute(value, axis, [(i, i ^ mask) for i in range(size)])


def bits_of(size):
    return [1 << b for b in range(size.bit_length() - 1)]


def exchange(value, axis):
    return lax.all_to_all(value, axis, split_axis=0, concat_axis=0, tiled=True)


ANY = pl.BlockSpec(memory_space=pl.ANY)
VMEM = pl.BlockSpec(memory_space=pltpu.VMEM)
SMEM = pl.BlockSpec(memory_space=pltpu.SMEM)


def call(body, outs, *args, specs=None, scratch=(), flops=0, moved=0):
    inner = body.func if isinstance(body, functools.partial) else body
    cost = pl.CostEstimate(flops=int(flops), bytes_accessed=2 * int(moved), transcendentals=0)
    return pl.pallas_call(
        body,
        out_shape=[jax.ShapeDtypeStruct(shape, kind) for shape, kind in outs],
        in_specs=[VMEM] * len(args) if specs is None else specs,
        out_specs=[VMEM] * len(outs),
        scratch_shapes=list(scratch),
        compiler_params=pltpu.CompilerParams(vmem_limit_bytes=VMEM_LIMIT),
        cost_estimate=cost if flops else None,
        name=inner.__name__,
    )(*args)


def shard_copies(me_ref, tp, own, parts, store, sems):
    copies = [own]
    for k in range(1, tp):
        group = []
        if len(parts) == 1:
            source = parts[0].at[me_ref[1] ^ k]
            group.append(pltpu.make_async_copy(source, store.at[k], sems.at[k, 0]))
        else:
            for core, part in enumerate(parts):
                rows = part.shape[1] // 4
                for chip in range(4):
                    source = part.at[k - 1, pl.ds(chip * rows, rows)]
                    target = store.at[k, me_ref[0] ^ (2 * chip + core)]
                    sem = sems.at[k, 2 * chip + core]
                    group.append(pltpu.make_async_copy(source, target, sem))
        copies.append(group)
    for group in copies:
        for copy in group:
            copy.start()

    def wait(k):
        for copy in copies[k]:
            copy.wait()

    return wait


def fetch(me_ref, tp, shard, parts, store, sems):
    own = [pltpu.make_async_copy(shard, store.at[0], sems.at[0, 0])]
    return shard_copies(me_ref, tp, own, parts, store, sems)


def relative_rows(me_ref, order, turned, store, count=None):
    if order is None:
        return turned
    store[...] = turned
    rows = turned.shape[0] >> len(order)
    picked = []
    for m in range(1 << len(order) if count is None else count):
        mask = sum(((m >> (len(order) - 1 - i)) & 1) << bit for i, bit in enumerate(order))
        start = pl.multiple_of((me_ref[0] ^ mask) * rows, rows)
        picked.append(store[pl.ds(start, rows), :])
    return jnp.concatenate(picked, axis=0)


def project(dims, me_ref, *refs):
    slots, ranks, few, tp, heads = dims
    blocks, (gain, weight, normed, pieces) = refs[:tp], refs[tp:]
    features = heads * HEAD
    part = slots * few
    pieces[heads * ranks :] = jnp.zeros_like(pieces[heads * ranks :])
    for k in range(tp):
        z = me_ref[1] ^ k
        value = blocks[k][...].astype(F32).reshape(slots, ranks, few, -1)
        value = jnp.concatenate(
            [value[c, r] for r in range(ranks) for c in range(slots)], axis=0
        )
        low = layer_norm(value, gain[...]).astype(BF)
        normed[z] = low
        columns = pl.ds(pl.multiple_of(z * part, part), part)
        proj = mm_nt(weight[...], low).astype(BF)
        for c in range(heads):
            for r in range(ranks):
                for t in range(3):
                    rows = t * features + c * HEAD
                    piece = proj[rows : rows + HEAD, r * part : (r + 1) * part]
                    pieces[c * ranks + r, t, :, columns] = piece


def tied_softmax(own, other, key_ok, scale):
    depth = own.shape[0] * own.shape[2]
    turned = own[:, 0].reshape(depth, -1).T
    logits = jnp.concatenate(
        [mm(turned, pair[:, 1].reshape(depth, -1)) for pair in (own, other)], axis=1
    )
    ok = key_ok[...] > 0
    masked = jnp.where(ok, logits * scale, NEGATIVE)
    powers = jnp.exp(masked - jnp.max(masked, axis=-1, keepdims=True))
    return masked, powers * (1.0 / jnp.sum(powers, axis=-1, keepdims=True)), ok


def attend(scale, own, other, key_ok, mixed):
    _, probs, _ = tied_softmax(own, other, key_ok, scale)
    depth = own.shape[0] * own.shape[2]
    low = probs.astype(BF)
    half = low.shape[1] // 2
    total = mm_nt(low[:, :half], own[:, 2].reshape(depth, -1))
    total += mm_nt(low[:, half:], other[:, 2].reshape(depth, -1))
    mixed[...] = total.astype(BF).reshape(mixed.shape)


def attend_back(scale, own, other, key_ok, weight, mixed_grad, query_grad, kept, given):
    masked, probs, ok = tied_softmax(own, other, key_ok, scale)
    seqs = own.shape[0]
    depth = seqs * own.shape[2]
    low = probs.astype(BF)
    half = low.shape[1] // 2
    out_grad = mixed_grad[...].reshape(-1, depth)
    prob_grad = jnp.concatenate(
        [mm(out_grad, pair[:, 2].reshape(depth, -1)) for pair in (own, other)], axis=1
    )
    prob_dot = jnp.sum(probs * prob_grad, axis=-1, keepdims=True)
    mean_logit = jnp.sum(jnp.where(ok, probs * masked, 0.0), axis=-1, keepdims=True)
    entropy = jnp.where(ok, probs * (masked - mean_logit), 0.0)
    grad = (probs * (prob_grad - prob_dot) - weight[...] * entropy).astype(BF)
    total = mm_nt(own[:, 1].reshape(depth, -1), grad[:, :half])
    total += mm_nt(other[:, 1].reshape(depth, -1), grad[:, half:])
    query_grad[...] = (total * scale).astype(BF).reshape(query_grad.shape)
    turned = out_grad.T
    flat = own[:, 0].reshape(depth, -1)
    shape = (seqs, HEAD, half)
    given[:, 0] = (mm(flat, grad[:, half:]) * scale).astype(BF).reshape(shape)
    given[:, 1] = mm(turned, low[:, half:]).astype(BF).reshape(shape)
    kept[:, 0] = (mm(flat, grad[:, :half]) * scale).reshape(shape)
    kept[:, 1] = mm(turned, low[:, :half]).reshape(shape)


def column_probs(query, key, rule, scale):
    scores = jnp.where(rule, mm_nt(query, key) * scale, NEGATIVE)
    powers = jnp.exp(scores - jnp.max(scores, axis=-1, keepdims=True))
    return powers * (1.0 / jnp.sum(powers, axis=-1, keepdims=True))


def same_column(count, few):
    rows = lax.broadcasted_iota(jnp.int32, (count, count), 0)
    columns = lax.broadcasted_iota(jnp.int32, (count, count), 1)
    return (rows % few) == (columns % few)


def narrow(store, k, features):
    whole = store[k].reshape(-1, store.shape[3])
    return [whole[i * features : (i + 1) * features] for i in range(5)]


def columns_forward(dims, parts, me_ref, both, arrived, gain, shard, *refs):
    few, tp, heads = dims
    parts, refs = refs[:parts], refs[parts:]
    after_row, normed, proj, right, after_col, store, sems = refs
    wait = fetch(me_ref, tp, shard, parts, store, sems)
    features = heads * HEAD
    seqs = both.shape[0]
    count = seqs * few
    total = both[:, 0].reshape(count, -1).astype(F32)
    attended = []
    for k in range(tp):
        z = me_ref[1] ^ k
        if len(arrived.shape) == 4:
            lanes = []
            for c in range(heads):
                value = arrived[z, c]
                pieces = [value[:, s * HEAD : (s + 1) * HEAD] for s in range(seqs)]
                lanes.append(jnp.concatenate(pieces, axis=0))
            attended.append(jnp.concatenate(lanes, axis=1))
        else:
            attended.append(arrived[z])
        right[k, :, 4 * features : 5 * features] = attended[k]
        right[k, :, 5 * features :] = jnp.zeros_like(right[k, :, 5 * features :])
    update = jnp.zeros_like(total)
    for k in range(tp):
        wait(k)
        update += mm(attended[k], narrow(store, k, features)[0])
    total = total + update
    after_row[...] = total
    low = layer_norm(total, gain[...]).astype(BF)
    normed[...] = low
    rule = same_column(count, few)
    update = jnp.zeros_like(total)
    for k in range(tp):
        weights = narrow(store, k, features)
        for t in range(3):
            proj[t, k] = mm_nt(low, weights[2 + t]).astype(BF)
        mixed = []
        for h in range(heads):
            at = slice(h * HEAD, (h + 1) * HEAD)
            probs = column_probs(proj[0, k, :, at], proj[1, k, :, at], rule, HEAD**-0.5)
            mixed.append(mm(probs.astype(BF), proj[2, k, :, at]).astype(BF))
        mixed = jnp.concatenate(mixed, axis=1)
        right[k, :, 3 * features : 4 * features] = mixed
        update += mm(mixed, weights[1])
    after_col[...] = total + update


def columns_backward(dims, parts, me_ref, *refs):
    few, tp, heads = dims
    middle, outputs, after_row, normed, proj, right, gain, shard = refs[:8]
    parts, refs = refs[8 : 8 + parts], refs[8 + parts :]
    home, left, right_out, row_mixed, gain_grad, store, sems = refs
    wait = fetch(me_ref, tp, shard, parts, store, sems)
    features = heads * HEAD
    count = middle.shape[0]
    seqs = count // few
    middle_low = middle[...].astype(BF)
    left[0] = normed[...]
    left[1] = middle_low
    rule = same_column(count, few)
    upstream = jnp.zeros(middle.shape, F32)
    for k in range(tp):
        wait(k)
        weights = narrow(store, k, features)
        mixed_grad = mm_nt(middle_low, weights[1]).astype(BF)
        grads = [[], [], []]
        for h in range(heads):
            at = slice(h * HEAD, (h + 1) * HEAD)
            query, key, value = proj[0, k, :, at], proj[1, k, :, at], proj[2, k, :, at]
            probs = column_probs(query, key, rule, HEAD**-0.5)
            out_grad = mixed_grad[:, at]
            prob_grad = mm_nt(out_grad, value)
            score = probs * (prob_grad - jnp.sum(probs * prob_grad, axis=-1, keepdims=True))
            score = score.astype(BF)
            grads[0].append((mm(score, key) * HEAD**-0.5).astype(BF))
            grads[1].append((mm(score.T, query) * HEAD**-0.5).astype(BF))
            grads[2].append(mm(probs.astype(BF).T, out_grad).astype(BF))
        for t in range(3):
            grad = jnp.concatenate(grads[t], axis=1)
            upstream += mm(grad, weights[2 + t])
            right_out[k, :, t * features : (t + 1) * features] = grad
        right_out[k, :, 3 * features :] = right[k, :, 3 * features :]
    back, gain_grad[...] = norm_back(after_row[...], gain[...], upstream)
    low = (middle[...] + back).astype(BF)
    home[:, 0] = outputs[...].reshape(seqs, few, -1)
    home[:, 1] = low.reshape(seqs, few, -1)
    left[2] = low
    for k in range(tp):
        z = me_ref[1] ^ k
        value = mm_nt(low, narrow(store, k, features)[0]).astype(BF)
        if len(row_mixed.shape) == 4:
            for c in range(heads):
                lane = value[:, c * HEAD : (c + 1) * HEAD]
                pieces = [lane[s * few : (s + 1) * few] for s in range(seqs)]
                row_mixed[z, c] = jnp.concatenate(pieces, axis=1)
            row_mixed[z, heads:] = jnp.zeros_like(row_mixed[z, heads:])
        else:
            row_mixed[z] = value


def store_halves(halves, z, value):
    rows = value.shape[0] // 2
    for half, part in zip(halves, (value[:rows], value[rows:])):
        half[:, z] = part.reshape(half.shape[0], half.shape[2], -1)


def column_weights(orders, me_ref, left, left_other, right, right_other, *refs):
    tp = right.shape[0]
    qkv, col_out, row_out, rows = refs[0:2], refs[2:4], refs[4:6], refs[6]
    features = col_out[0].shape[3]
    turned = []
    for i in range(3):
        value = jnp.concatenate([left[i], left_other[i]], axis=0).T
        turned.append(relative_rows(me_ref, orders[i], value, rows.at[i], 4))
    for k in range(tp):
        value = jnp.concatenate([right[k], right_other[k]], axis=0)
        start = 0
        for i, (halves, size) in enumerate(((qkv, 3), (col_out, 1), (row_out, 1))):
            columns = slice(start, start + size * features)
            store_halves(halves, me_ref[1] ^ k, mm(turned[i], value[:, columns]).astype(BF))
            start += size * features


def wide_weights(orders, me_ref, left, left_other, right, right_other, *refs):
    rows = refs[4]
    for i, grads in enumerate((refs[0:2], refs[2:4])):
        value = jnp.concatenate([left[i], left_other[i]], axis=0).T
        turned = relative_rows(me_ref, orders[i], value, rows.at[i], 4)
        for k in range(right.shape[1]):
            both = jnp.concatenate([right[i, k], right_other[i, k]], axis=0)
            store_halves(grads, me_ref[1] ^ k, mm(turned, both).astype(BF))


def feed_forward(tp, parts, me_ref, after_col, arrived, gain, up_shard, down_shard, *refs):
    parts, refs = refs[:parts], refs[parts:]
    outputs, middle, gain_grad, left, right, store, sems = refs
    half = store.shape[1] // 2
    own = [
        pltpu.make_async_copy(up_shard, store.at[0, pl.ds(0, half)], sems.at[0, 0]),
        pltpu.make_async_copy(down_shard, store.at[0, pl.ds(half, half)], sems.at[0, 1]),
    ]
    wait = shard_copies(me_ref, tp, own, parts, store, sems)
    value = after_col[...]
    low = layer_norm(value, gain[...]).astype(BF)
    given = arrived[:, 1].reshape(value.shape)
    left[0] = low
    left[1] = given
    result = value
    upstream = jnp.zeros_like(value)
    for k in range(tp):
        wait(k)
        up = store[k, :half].reshape(-1, store.shape[3])
        down = store[k, half:].reshape(-1, store.shape[3])
        hidden, slope = gelu_parts(mm(low, up))
        hidden = hidden.astype(BF)
        right[1, k] = hidden
        result += mm(hidden, down)
        pre_grad = (mm_nt(given, down) * slope).astype(BF)
        right[0, k] = pre_grad
        upstream += mm_nt(pre_grad, up)
    outputs[...] = result.astype(BF)
    back, gain_grad[...] = norm_back(value, gain[...], upstream)
    middle[...] = given.astype(F32) + back


def gather_grads(dims, order, me_ref, back, normed, gain, weight, *outs):
    slots, ranks, few, tp, heads = dims
    features = heads * HEAD
    part = slots * few
    pieces, kept, sent, gain_grad, rows = outs
    total = jnp.zeros((3 * features, normed.shape[2]), F32)
    for k in range(tp):
        z = me_ref[1] ^ k
        columns = pl.ds(pl.multiple_of(z * part, part), part)
        for c in range(heads):
            for r in range(ranks):
                for t in range(3):
                    piece = back[c * ranks + r, t, :, columns]
                    at = t * features + c * HEAD
                    pieces[z, at : at + HEAD, r * part : (r + 1) * part] = piece
        total += mm(pieces[z], normed[z])
    gain_grad[...] = (
        jnp.sum(total * weight[...].astype(F32), axis=0, keepdims=True) / gain[...]
    )
    turned = relative_rows(me_ref, order, total.T.astype(BF), rows)
    half = turned.shape[0] // 2
    kept[...] = turned[:half].reshape(kept.shape)
    sent[...] = turned[half:].reshape(sent.shape)


def finish(dims, parts, me_ref, *refs):
    slots, ranks, few, tp, heads = dims
    features = heads * HEAD
    pieces, tokens, gain, home, shard = refs[:5]
    parts, (result, store, sems) = refs[5 : 5 + parts], refs[5 + parts :]
    wait = fetch(me_ref, tp, shard, parts, store, sems)
    inner = home[:, few : 2 * few].reshape(tokens.shape)
    upstream = jnp.zeros(inner.shape, F32)
    for k in range(tp):
        wait(k)
        whole = store[k].reshape(-1, store.shape[3])[: 3 * features]
        upstream += mm(pieces[me_ref[1] ^ k].T, whole)
    upstream = upstream.reshape(ranks, slots, few, -1)
    upstream = jnp.concatenate(
        [upstream[r, c] for c in range(slots) for r in range(ranks)], axis=0
    )
    back, _ = norm_back(tokens[...].astype(F32), gain[...], upstream)
    result[...] = (inner.astype(F32) + back).astype(BF)


def after(value, *others):
    return lax.optimization_barrier((value,) + others)[0]


def together(*values):
    return lax.optimization_barrier(values)


def two_terms(gains):
    high = lax.reduce_precision(gains, 8, 7)
    low = gains - high
    return jnp.pad(jnp.concatenate([high, low], axis=0), ((0, 10), (0, 0))).astype(BF)


def one_term(rows):
    return rows[:3] + rows[3:6]


def add(left, right):
    return (left.astype(F32) + right.astype(F32)).astype(BF)


def local(
    tokens,
    cotangent,
    lengths,
    column_mask,
    row_gain,
    row_qkv,
    row_out,
    col_gain,
    col_qkv,
    col_out,
    ffn_gain,
    ffn_up,
    ffn_down,
):
    slots, ranks, tp = lax.axis_size("c"), lax.axis_size("r"), lax.axis_size("tp")
    seqs = slots * ranks
    block, width = tokens.shape[2], tokens.shape[3]
    cols = column_mask.shape[1]
    few = block // seqs
    part = slots * few
    features = row_qkv.shape[2]
    heads = features // HEAD
    hidden = ffn_up.shape[1]
    queries = tp * part
    count = seqs * few
    tied_scale = (HEAD * seqs) ** (-0.5)
    my_seq, my_rank, my_z = lax.axis_index(SEQ), lax.axis_index("r"), lax.axis_index("tp")
    me_ref = jnp.stack([my_seq, my_z]).astype(jnp.int32)
    dims = (slots, ranks, few, tp, heads)
    fast = seqs == 8 and ranks == 2
    row_gain, col_gain, ffn_gain = row_gain[None], col_gain[None], ffn_gain[None]

    penalty_scale = ENTROPY_WEIGHT * (seqs * cols) / (HEADS * jnp.sum(lengths).astype(F32))
    position = jnp.arange(cols, dtype=jnp.int32).reshape(tp, slots, ranks, few)
    position = position.transpose(2, 0, 1, 3)
    flag = column_mask.reshape(tp, slots, ranks, few).transpose(2, 0, 1, 3)
    valid = (position < lengths[0]) & ((flag == 1) | (position == 0))
    valid = valid.astype(F32).reshape(ranks, queries)
    key_ok = jnp.concatenate(
        [lax.dynamic_index_in_dim(valid, my_rank ^ k, 0) for k in range(ranks)], axis=1
    )
    query_position = lax.dynamic_index_in_dim(position.reshape(ranks, queries), my_rank, 0)
    query_weight = jnp.where(query_position < lengths[0], penalty_scale, 0.0).reshape(queries, 1)

    own = tokens[0, 0]
    both = [value.reshape(seqs, few, width) for value in (own, cotangent[0, 0])]
    both = jnp.stack(both, axis=1)

    row_weight = row_qkv.transpose(0, 2, 1).reshape(3 * features, width)
    shard_a = jnp.concatenate(
        [row_out, col_out, col_qkv.transpose(0, 2, 1).reshape(3 * features, width)]
    )

    def cut(shard, least):
        rows = shard.shape[0]
        rows += -rows % (seqs * least)
        shard = jnp.pad(shard, ((0, rows - shard.shape[0]), (0, 0)))
        return shard.reshape(seqs, rows // seqs, width)

    shard_a = cut(shard_a, 16 if fast else 1)
    shard_c = cut(row_weight, 16 if fast else 1)
    shard_b = cut(jnp.concatenate([ffn_up, ffn_down]), 1)

    def mine(shard):
        return lax.dynamic_index_in_dim(shard, my_seq, 0, keepdims=False)

    def along_tp(piece):
        return jnp.stack([swap(piece, "tp", tp, k) for k in range(1, tp)])

    def along_plane(held):
        return [swap(held, "c", slots, mask) for mask in (1, 2)]

    def across_plane(near):
        half = near[0].shape[1] // 2
        one = swap(near[0][:, :half], "c", slots, 2)
        return [one, swap(near[1][:, half:], "c", slots, 1)]

    def along_cores(parts):
        held = jnp.concatenate(parts, axis=1)
        return [held, swap(held, "r", ranks, 1)]

    def blocks_of(value):
        return [own] + [swap(value, "tp", tp, k) for k in range(1, tp)]

    if fast:
        near_a = along_tp(mine(shard_a))
        sent, both, near_a = together(own, both, near_a)
        blocks = blocks_of(sent)
        both = exchange(both, SEQ)
        plane_a = along_plane(near_a)
        blocks[1], blocks[2], blocks[3], both, *plane_a = together(*blocks[1:], both, *plane_a)
        near_b = along_tp(after(mine(shard_b), blocks[1]))
    else:
        blocks = blocks_of(own)
        both = exchange(both, SEQ)

        def everywhere(shard):
            rows = shard.shape[0] * shard.shape[1]
            whole = lax.all_gather(mine(shard), ("tp",) + SEQ, axis=0)
            return [whole.reshape(tp, 8, rows // 8, width)]

        parts_a, parts_b, parts_c = everywhere(shard_a), everywhere(shard_b), everywhere(shard_c)
        shard_a = shard_a.reshape(8, -1, width)
        shard_c = shard_c.reshape(8, -1, width)
    up_own = ffn_up.reshape(4, -1, width)
    down_own = ffn_down.reshape(4, -1, width)
    store_a = pltpu.VMEM((tp,) + shard_a.shape, BF)
    store_b = pltpu.VMEM((tp, 8, shard_b.shape[0] * shard_b.shape[1] // 8, width), BF)
    store_c = pltpu.VMEM((tp,) + shard_c.shape, BF)
    sems = pltpu.SemaphoreType.DMA((tp, 10))

    if fast:
        normed, pieces = call(
            functools.partial(project, dims),
            [((tp, block, width), BF), ((seqs, 3, HEAD, queries), BF)],
            me_ref,
            *blocks,
            row_gain,
            row_weight,
            specs=[SMEM] + [VMEM] * (tp + 2),
            flops=2 * cols * width * 3 * features,
            moved=8 << 20,
        )
    else:
        order = jnp.stack(blocks)[my_z ^ jnp.arange(tp)]
        order = order.reshape(tp, slots, ranks, few, width).transpose(0, 2, 1, 3, 4)
        normed = layer_norm(order.astype(F32), row_gain).astype(BF).reshape(tp, block, width)
        pieces = jnp.einsum("fd,zld->fzl", row_weight, normed, preferred_element_type=F32)
        pieces = pieces.astype(BF).reshape(3, heads, HEAD, tp, ranks, part)
        pieces = pieces.transpose(1, 4, 0, 2, 3, 5).reshape(heads, ranks, 3, HEAD, queries)
        pieces = jnp.pad(pieces, ((0, slots - heads),) + ((0, 0),) * 4)
        pieces = pieces.reshape(seqs, 3, HEAD, queries)
    if fast:
        pieces, *plane_a = together(pieces, *plane_a)
        cross_a = across_plane(plane_a)
    pieces = exchange(pieces, SEQ)
    mixed_shape = (tp * slots, few, seqs * HEAD)
    if fast:
        pieces, near_b, *cross_a = together(pieces, near_b, *cross_a)
        others = swap(pieces, "r", ranks, 1)
        others, near_b = together(others, near_b)
        plane_b = along_plane(near_b)
        parts_a = along_cores([near_a] + plane_a + cross_a)
        (mixed,) = call(
            functools.partial(attend, tied_scale),
            [(mixed_shape, BF)],
            pieces,
            others,
            key_ok,
            flops=4 * cols * queries * seqs * HEAD,
            moved=8 << 20,
        )
    else:
        pairs = lax.all_gather(pieces[:, 1:], "r", axis=0)
        pairs = pairs.transpose(2, 1, 3, 0, 4).reshape(2, seqs * HEAD, cols)
        key, value = pairs[0], pairs[1]
        query = pieces[:, 0].reshape(seqs * HEAD, queries)
        key_ok = valid.reshape(1, cols)
        logits = jnp.einsum("ki,kj->ij", query, key, preferred_element_type=F32) * tied_scale
        masked = jnp.where(key_ok > 0, logits, NEGATIVE)
        powers = jnp.exp(masked - jnp.max(masked, axis=-1, keepdims=True))
        probs = powers / jnp.sum(powers, axis=-1, keepdims=True)
        mixed = jnp.einsum("ij,kj->ik", probs.astype(BF), value, preferred_element_type=F32)
        mixed = mixed.astype(BF).reshape(mixed_shape)
    if fast:
        mixed, parts_a[1], *plane_b = together(mixed, parts_a[1], *plane_b)
        cross_b = across_plane(plane_b)
    mixed = exchange(mixed, ("tp", "c"))
    shards = (tp, count, features)
    if fast:
        mixed, *cross_b = together(mixed, *cross_b)
        arrived = mixed.reshape(tp, slots, few, seqs * HEAD)
        parts_b = along_cores([near_b] + plane_b + cross_b)
        near_c = along_tp(after(mine(shard_c), mixed))
    else:
        arrived = (
            mixed.reshape(tp, slots, few, seqs, HEAD)[:, :heads]
            .transpose(0, 3, 2, 1, 4)
            .reshape(shards)
        )

    flat = (count, width)
    packed = (tp, count, 5 * features + -5 * features % 128)
    n_parts = len(parts_a)
    after_row, col_normed, col_proj, col_right, after_col = call(
        functools.partial(columns_forward, (few, tp, heads), n_parts),
        [(flat, F32), (flat, BF), ((3,) + shards, BF), (packed, BF), (flat, F32)],
        me_ref,
        both,
        arrived,
        col_gain,
        shard_a,
        *parts_a,
        specs=[SMEM] + [VMEM] * 3 + [ANY] * (1 + n_parts),
        scratch=[store_a, sems],
        flops=2 * count * width * width * 5,
        moved=20 << 20,
    )
    if fast:
        after_col, near_c = together(after_col, near_c)
        plane_c = along_plane(near_c)
    outputs, middle, ffn_gain_grad, wide_left, wide_right = call(
        functools.partial(feed_forward, tp, n_parts),
        [
            (flat, BF),
            (flat, F32),
            ((1, width), F32),
            ((2,) + flat, BF),
            ((2, tp, count, hidden), BF),
        ],
        me_ref,
        after_col,
        both,
        ffn_gain,
        up_own,
        down_own,
        *parts_b,
        specs=[SMEM] + [VMEM] * 3 + [ANY] * (2 + n_parts),
        scratch=[store_b, sems],
        flops=2 * count * width * hidden * tp * 4,
        moved=30 << 20,
    )
    home, col_left, col_right, row_mixed, col_gain_grad = call(
        functools.partial(columns_backward, (few, tp, heads), n_parts),
        [
            ((seqs, 2, few, width), BF),
            ((3,) + flat, BF),
            (packed, BF),
            ((tp, slots, few, seqs * HEAD) if fast else shards, BF),
            ((1, width), F32),
        ],
        me_ref,
        middle,
        outputs,
        after_row,
        col_normed,
        col_proj,
        col_right,
        col_gain,
        shard_a,
        *parts_a,
        specs=[SMEM] + [VMEM] * 7 + [ANY] * (1 + n_parts),
        scratch=[store_a, sems],
        flops=2 * count * width * width * 8,
        moved=30 << 20,
    )

    def halve(kept, came):
        half = kept.shape[0] // 2
        return add(kept[:half], came[:half]), add(kept[half:], came[half:])

    def give(sent, mask):
        return swap(sent, "c", slots, mask)

    def last(held):
        return jnp.sum(exchange(held, "tp").astype(F32), axis=0)

    def all_at_once(left, right):
        grad = jnp.einsum("ld,zlf->zdf", left, right, preferred_element_type=F32).astype(BF)
        grad = lax.psum_scatter(grad, SEQ, scatter_dimension=1, tiled=True)
        return lax.psum_scatter(grad, "tp", scatter_dimension=0, tiled=True)[0].astype(F32)

    rows_of = width // seqs
    turned_rows = pltpu.VMEM((3, width, 2 * count), BF)
    if fast:
        wide_others = swap(wide_left, "r", ranks, 1), swap(wide_right, "r", ranks, 1)
        col_others = swap(col_left, "r", ranks, 1), swap(col_right, "r", ranks, 1)
        up_kept, up_sent, down_kept, down_sent = call(
            functools.partial(wide_weights, ((0, 2, 1), (0, 1, 2))),
            [((2, tp, rows_of, hidden), BF)] * 4,
            me_ref,
            wide_left,
            wide_others[0],
            wide_right,
            wide_others[1],
            specs=[SMEM] + [VMEM] * 4,
            scratch=[turned_rows],
            flops=2 * count * width * hidden * tp * 2,
            moved=30 << 20,
        )
        qkv_kept, qkv_sent, *outs_halves = call(
            functools.partial(column_weights, ((0, 2, 1), (0, 1, 2), (0, 1, 2))),
            [((2, tp, rows_of, 3 * features), BF)] * 2
            + [((2, tp, rows_of, features), BF)] * 4,
            me_ref,
            after(col_left, up_sent),
            col_others[0],
            col_right,
            col_others[1],
            specs=[SMEM] + [VMEM] * 4,
            scratch=[turned_rows],
            flops=2 * count * width * width * 5,
            moved=12 << 20,
        )
    else:
        row_mixed = row_mixed.reshape(tp, seqs, few, heads, HEAD).transpose(0, 3, 2, 1, 4)
        row_mixed = jnp.pad(row_mixed, ((0, 0), (0, slots - heads)) + ((0, 0),) * 3)
        my_order = my_z ^ jnp.arange(tp)
        col_right = col_right[my_order]
    row_mixed = exchange(row_mixed.reshape(mixed_shape), ("tp", "c"))
    if fast:
        up_sent, down_sent, *plane_c = together(up_sent, down_sent, *plane_c)
        up_came, down_came = give(up_sent, 2), give(down_sent, 1)
        row_mixed = after(row_mixed, qkv_sent)
        query_grad, kept, sent = call(
            functools.partial(attend_back, tied_scale),
            [
                ((seqs, HEAD, queries), BF),
                ((seqs, 2, HEAD, queries), F32),
                ((seqs, 2, HEAD, queries), BF),
            ],
            pieces,
            others,
            key_ok,
            query_weight,
            row_mixed,
            flops=10 * cols * queries * seqs * HEAD,
            moved=16 << 20,
        )
        sent = after(sent, up_came, down_came)
        pair_grad = (kept + swap(sent, "r", ranks, 1).astype(F32)).astype(BF)
        (up_kept, up_sent), (down_kept, down_sent) = halve(up_kept, up_came), halve(down_kept, down_came)
        up_came, down_came = give(up_sent, 1), give(down_sent, 2)
        back = jnp.concatenate([query_grad[:, None], pair_grad], axis=1)
        back, up_came, down_came = together(back, up_came, down_came)
        wide_last = jnp.concatenate(
            [add(up_kept, up_came)[0], add(down_kept, down_came)[0]], axis=-1
        )
        wide_came = [
            swap(lax.dynamic_index_in_dim(wide_last, my_z ^ k, keepdims=False), "tp", tp, k)
            for k in range(1, tp)
        ]
    else:
        out_grad = row_mixed.reshape(queries, seqs * HEAD)
        prob_grad = jnp.einsum("ik,kj->ij", out_grad, value, preferred_element_type=F32)
        prob_dot = jnp.sum(probs * prob_grad, axis=-1, keepdims=True)
        mean_logit = jnp.sum(
            jnp.where(key_ok > 0, probs * masked, 0.0), axis=-1, keepdims=True
        )
        entropy = jnp.where(key_ok > 0, probs * (masked - mean_logit), 0.0)
        grad = (probs * (prob_grad - prob_dot) - query_weight * entropy).astype(BF)
        total = jnp.einsum("ij,kj->ki", grad, key, preferred_element_type=F32)
        query_grad = (total * tied_scale).astype(BF).reshape(seqs, HEAD, queries)
        key_grad = jnp.einsum("ki,ij->kj", query, grad, preferred_element_type=F32)
        value_grad = jnp.einsum(
            "ik,ij->kj", out_grad, probs.astype(BF), preferred_element_type=F32
        )
        both = jnp.stack([(key_grad * tied_scale).astype(BF), value_grad.astype(BF)])
        both = both.reshape(2, seqs, HEAD, ranks, queries).transpose(3, 1, 0, 2, 4)
        pair_grad = lax.psum_scatter(both, "r", scatter_dimension=0, tiled=False)
        back = jnp.concatenate([query_grad[:, None], pair_grad], axis=1)
    back = exchange(back, SEQ)
    if fast:
        col_out_kept, col_out_sent, row_out_kept, row_out_sent = outs_halves
        outs_kept = jnp.concatenate([col_out_kept, row_out_kept], axis=3)
        outs_sent = jnp.concatenate([col_out_sent, row_out_sent], axis=3)
        qkv_sent, outs_sent, back, *rest = together(qkv_sent, outs_sent, back, *plane_c, *wide_came)
        plane_c, wide_came = rest[:2], rest[2:]
        qkv_came, outs_came = give(qkv_sent, 2), give(outs_sent, 1)
        wide_grad = lax.dynamic_index_in_dim(wide_last, my_z, keepdims=False).astype(F32)
        for value in wide_came:
            wide_grad = wide_grad + value.astype(F32)
        parts_c = along_cores([near_c] + plane_c + across_plane(plane_c))
        traded, kept, sent, row_gain_grad = call(
            functools.partial(gather_grads, dims, (0, 2, 1)),
            [((tp, 3 * features, block), BF)]
            + [((4, rows_of, 3 * features), BF)] * 2
            + [((1, width), F32)],
            me_ref,
            back,
            normed,
            row_gain,
            row_weight,
            specs=[SMEM] + [VMEM] * 4,
            scratch=[pltpu.VMEM((width, 3 * features), BF)],
            flops=2 * cols * width * 3 * features,
            moved=8 << 20,
        )
    else:
        both = back.reshape(slots, ranks, 3, HEAD, tp, part)[:heads]
        both = both.transpose(4, 2, 0, 3, 1, 5).reshape(tp, 3 * features, block)
        row_grad = jnp.einsum("zld,zfl->df", normed, both, preferred_element_type=F32)
        row_gain_grad = (
            jnp.sum(row_grad.T * row_weight.astype(F32), axis=0, keepdims=True) / row_gain
        )
        traded = both
    gains = jnp.concatenate([row_gain_grad, col_gain_grad, ffn_gain_grad], axis=0)
    home = home.reshape(seqs, 2 * few, width)
    if fast:
        traded = exchange(traded, "tp")
        came = swap(sent, "r", ranks, 1)
        home, traded, qkv_came, outs_came, came = together(home, traded, qkv_came, outs_came, came)
        (qkv_kept, qkv_sent), (outs_kept, outs_sent) = halve(qkv_kept, qkv_came), halve(outs_kept, outs_came)
        qkv_came, outs_came = give(qkv_sent, 1), give(outs_sent, 2)
        ends = jnp.broadcast_to(two_terms(gains), (seqs, 16, width))
        home = exchange(jnp.concatenate([home, ends], axis=1), SEQ)
        gains = one_term(jnp.sum(home[:, 2 * few :].astype(F32), axis=0))
        kept, sent = add(kept[:2], came[:2]), add(kept[2:], came[2:])
        kept, sent = halve(kept, give(sent, 2))
        row_grad = add(kept[0], give(sent, 1)[0]).astype(F32)
        small = jnp.concatenate(
            [add(qkv_kept, qkv_came)[0], add(outs_kept, outs_came)[0]], axis=-1
        )
        ends = jnp.pad(two_terms(gains), ((0, 0), (0, small.shape[2] - width)))
        ends = jnp.broadcast_to(ends, (tp,) + ends.shape)
        small = last(jnp.concatenate([small, ends], axis=1))
        gains = one_term(small[rows_of:, :width])
        small = small[:rows_of]
        qkv, outs = small[:, : 3 * features], small[:, 3 * features :]
        up_grad, down_grad = wide_grad[:, :hidden], wide_grad[:, hidden:]
    else:
        traded = exchange(traded, "tp")
        home = exchange(home, SEQ)
        for axis, size in (("r", ranks), ("c", slots), ("tp", tp)):
            for k in bits_of(size):
                gains = gains + swap(gains, axis, size, k)
    outputs = home[:, :few].reshape(block, width)
    (input_grad,) = call(
        functools.partial(finish, dims, n_parts),
        [((block, width), BF)],
        me_ref,
        traded,
        own,
        row_gain,
        home,
        shard_c,
        *parts_c,
        specs=[SMEM] + [VMEM] * 4 + [ANY] * (1 + n_parts),
        scratch=[store_c, sems],
        flops=2 * block * width * width * 3,
        moved=8 << 20,
    )
    if not fast:
        row_grad = lax.psum_scatter(row_grad, SEQ, scatter_dimension=0, tiled=True)
        wide_right = wide_right[:, my_order]
        up_grad = all_at_once(wide_left[0], wide_right[0])
        down_grad = all_at_once(wide_left[1], wide_right[1])
        qkv = all_at_once(col_left[0], col_right[..., : 3 * features])
        outs = jnp.concatenate(
            [
                all_at_once(col_left[1], col_right[..., 3 * features : 4 * features]),
                all_at_once(col_left[2], col_right[..., 4 * features : 5 * features]),
            ],
            axis=1,
        )

    def thirds(value):
        return value.reshape(width // seqs, 3, features).transpose(1, 0, 2)

    return (
        outputs[None, None],
        input_grad[None, None],
        gains[0],
        thirds(row_grad),
        outs[:, features:].T,
        gains[1],
        thirds(qkv),
        outs[:, :features].T,
        gains[2],
        up_grad,
        down_grad.T,
    )


def solution(mesh):
    seqs, tp = mesh.shape["seq"], mesh.shape["tp"]
    heads = HEADS // tp
    slots = 1 << (heads - 1).bit_length()
    split = Mesh(mesh.devices.reshape(slots, seqs // slots, tp), ("c", "r", "tp"))
    return jax.shard_map(
        local,
        mesh=split,
        in_specs=(
            P(None, SEQ, "tp", None),
            P(None, SEQ, "tp", None),
            P(),
            P(),
            P(),
            P(None, None, "tp"),
            P("tp", None),
            P(),
            P(None, None, "tp"),
            P("tp", None),
            P(),
            P(None, "tp"),
            P("tp", None),
        ),
        out_specs=(
            P(None, SEQ, "tp", None),
            P(None, SEQ, "tp", None),
            P(),
            P(None, SEQ, "tp"),
            P("tp", SEQ),
            P(),
            P(None, SEQ, "tp"),
            P("tp", SEQ),
            P(),
            P(SEQ, "tp"),
            P("tp", SEQ),
        ),
        check_vma=False,
    )
```

```python
import functools

import jax
import jax.numpy as jnp
from jax import lax
from jax.experimental import pallas as pl
from jax.experimental.pallas import tpu as pltpu
from jax.sharding import Mesh
from jax.sharding import PartitionSpec as P

HEADS = 12
HEAD = 64
EPSILON = 1e-05
NEGATIVE = -1e30
ENTROPY_WEIGHT = 4.0

SEQ = ("c", "r")
BF = jnp.bfloat16
F32 = jnp.float32
VMEM_LIMIT = 60 * 1024 * 1024


def statistics(value):
    average = jnp.mean(value, axis=-1, keepdims=True)
    centred = value - average
    inverse = lax.rsqrt(jnp.mean(centred * centred, axis=-1, keepdims=True) + EPSILON)
    return centred * inverse, inverse


def layer_norm(value, gain):
    unit, _ = statistics(value)
    return unit * gain


def norm_back(value, gain, upstream):
    unit, inverse = statistics(value)
    scaled = upstream * gain
    back = inverse * (
        scaled
        - jnp.mean(scaled, axis=-1, keepdims=True)
        - unit * jnp.mean(scaled * unit, axis=-1, keepdims=True)
    )
    return back, jnp.sum(upstream * unit, axis=0, keepdims=True)


def gelu_parts(value):
    share = 0.5 * (1.0 + lax.erf(value * (0.5**0.5)))
    slope = share + value * jnp.exp(-0.5 * value * value) * 0.3989422804014327
    return value * share, slope


def mm(left, right):
    return lax.dot_general(left, right, (((1,), (0,)), ((), ())), preferred_element_type=F32)


def mm_nt(left, right):
    return lax.dot_general(left, right, (((1,), (1,)), ((), ())), preferred_element_type=F32)


def swap(value, axis, size, mask):
    return lax.ppermute(value, axis, [(i, i ^ mask) for i in range(size)])


def bits_of(size):
    return [1 << b for b in range(size.bit_length() - 1)]


def exchange(value, axis):
    return lax.all_to_all(value, axis, split_axis=0, concat_axis=0, tiled=True)


ANY = pl.BlockSpec(memory_space=pl.ANY)
VMEM = pl.BlockSpec(memory_space=pltpu.VMEM)
SMEM = pl.BlockSpec(memory_space=pltpu.SMEM)


def call(body, outs, *args, specs=None, scratch=(), flops=0, moved=0):
    inner = body.func if isinstance(body, functools.partial) else body
    cost = pl.CostEstimate(flops=int(flops), bytes_accessed=2 * int(moved), transcendentals=0)
    return pl.pallas_call(
        body,
        out_shape=[jax.ShapeDtypeStruct(shape, kind) for shape, kind in outs],
        in_specs=[VMEM] * len(args) if specs is None else specs,
        out_specs=[VMEM] * len(outs),
        scratch_shapes=list(scratch),
        compiler_params=pltpu.CompilerParams(vmem_limit_bytes=VMEM_LIMIT),
        cost_estimate=cost if flops else None,
        name=inner.__name__,
    )(*args)


def shard_copies(me_ref, tp, own, parts, store, sems):
    copies = [own]
    for k in range(1, tp):
        group = []
        if len(parts) == 1:
            source = parts[0].at[me_ref[1] ^ k]
            group.append(pltpu.make_async_copy(source, store.at[k], sems.at[k, 0]))
        else:
            for core, part in enumerate(parts):
                rows = part.shape[1] // 4
                for chip in range(4):
                    source = part.at[k - 1, pl.ds(chip * rows, rows)]
                    target = store.at[k, me_ref[0] ^ (2 * chip + core)]
                    sem = sems.at[k, 2 * chip + core]
                    group.append(pltpu.make_async_copy(source, target, sem))
        copies.append(group)
    for group in copies:
        for copy in group:
            copy.start()

    def wait(k):
        for copy in copies[k]:
            copy.wait()

    return wait


def fetch(me_ref, tp, shard, parts, store, sems):
    own = [pltpu.make_async_copy(shard, store.at[0], sems.at[0, 0])]
    return shard_copies(me_ref, tp, own, parts, store, sems)


def relative_rows(me_ref, order, turned, store, count=None):
    if order is None:
        return turned
    store[...] = turned
    rows = turned.shape[0] >> len(order)
    picked = []
    for m in range(1 << len(order) if count is None else count):
        mask = sum(((m >> (len(order) - 1 - i)) & 1) << bit for i, bit in enumerate(order))
        start = pl.multiple_of((me_ref[0] ^ mask) * rows, rows)
        picked.append(store[pl.ds(start, rows), :])
    return jnp.concatenate(picked, axis=0)


def project(dims, me_ref, *refs):
    slots, ranks, few, tp, heads = dims
    blocks, (gain, weight, normed, pieces) = refs[:tp], refs[tp:]
    features = heads * HEAD
    part = slots * few
    pieces[heads * ranks :] = jnp.zeros_like(pieces[heads * ranks :])
    for k in range(tp):
        z = me_ref[1] ^ k
        value = blocks[k][...].astype(F32).reshape(slots, ranks, few, -1)
        value = jnp.concatenate(
            [value[c, r] for r in range(ranks) for c in range(slots)], axis=0
        )
        low = layer_norm(value, gain[...]).astype(BF)
        normed[z] = low
        columns = pl.ds(pl.multiple_of(z * part, part), part)
        proj = mm_nt(weight[...], low).astype(BF)
        for c in range(heads):
            for r in range(ranks):
                for t in range(3):
                    rows = t * features + c * HEAD
                    piece = proj[rows : rows + HEAD, r * part : (r + 1) * part]
                    pieces[c * ranks + r, t, :, columns] = piece


def tied_softmax(own, other, key_ok, scale):
    depth = own.shape[0] * own.shape[2]
    turned = own[:, 0].reshape(depth, -1).T
    logits = jnp.concatenate(
        [mm(turned, pair[:, 1].reshape(depth, -1)) for pair in (own, other)], axis=1
    )
    ok = key_ok[...] > 0
    masked = jnp.where(ok, logits * scale, NEGATIVE)
    powers = jnp.exp(masked - jnp.max(masked, axis=-1, keepdims=True))
    return masked, powers * (1.0 / jnp.sum(powers, axis=-1, keepdims=True)), ok


def attend(scale, own, other, key_ok, mixed):
    _, probs, _ = tied_softmax(own, other, key_ok, scale)
    depth = own.shape[0] * own.shape[2]
    low = probs.astype(BF)
    half = low.shape[1] // 2
    total = mm_nt(low[:, :half], own[:, 2].reshape(depth, -1))
    total += mm_nt(low[:, half:], other[:, 2].reshape(depth, -1))
    mixed[...] = total.astype(BF).reshape(mixed.shape)


def attend_back(scale, own, other, key_ok, weight, mixed_grad, query_grad, kept, given):
    masked, probs, ok = tied_softmax(own, other, key_ok, scale)
    seqs = own.shape[0]
    depth = seqs * own.shape[2]
    low = probs.astype(BF)
    half = low.shape[1] // 2
    out_grad = mixed_grad[...].reshape(-1, depth)
    prob_grad = jnp.concatenate(
        [mm(out_grad, pair[:, 2].reshape(depth, -1)) for pair in (own, other)], axis=1
    )
    prob_dot = jnp.sum(probs * prob_grad, axis=-1, keepdims=True)
    mean_logit = jnp.sum(jnp.where(ok, probs * masked, 0.0), axis=-1, keepdims=True)
    entropy = jnp.where(ok, probs * (masked - mean_logit), 0.0)
    grad = (probs * (prob_grad - prob_dot) - weight[...] * entropy).astype(BF)
    total = mm_nt(own[:, 1].reshape(depth, -1), grad[:, :half])
    total += mm_nt(other[:, 1].reshape(depth, -1), grad[:, half:])
    query_grad[...] = (total * scale).astype(BF).reshape(query_grad.shape)
    turned = out_grad.T
    flat = own[:, 0].reshape(depth, -1)
    shape = (seqs, HEAD, half)
    given[:, 0] = (mm(flat, grad[:, half:]) * scale).astype(BF).reshape(shape)
    given[:, 1] = mm(turned, low[:, half:]).astype(BF).reshape(shape)
    kept[:, 0] = (mm(flat, grad[:, :half]) * scale).reshape(shape)
    kept[:, 1] = mm(turned, low[:, :half]).reshape(shape)


def column_probs(query, key, rule, scale):
    scores = jnp.where(rule, mm_nt(query, key) * scale, NEGATIVE)
    powers = jnp.exp(scores - jnp.max(scores, axis=-1, keepdims=True))
    return powers * (1.0 / jnp.sum(powers, axis=-1, keepdims=True))


def same_column(count, few):
    rows = lax.broadcasted_iota(jnp.int32, (count, count), 0)
    columns = lax.broadcasted_iota(jnp.int32, (count, count), 1)
    return (rows % few) == (columns % few)


def narrow(store, k, features):
    whole = store[k].reshape(-1, store.shape[3])
    return [whole[i * features : (i + 1) * features] for i in range(5)]


def columns_forward(dims, parts, me_ref, both, arrived, gain, shard, *refs):
    few, tp, heads = dims
    parts, refs = refs[:parts], refs[parts:]
    after_row, normed, proj, right, after_col, store, sems = refs
    wait = fetch(me_ref, tp, shard, parts, store, sems)
    features = heads * HEAD
    seqs = both.shape[0]
    count = seqs * few
    total = both[:, 0].reshape(count, -1).astype(F32)
    attended = []
    for k in range(tp):
        z = me_ref[1] ^ k
        if len(arrived.shape) == 4:
            lanes = []
            for c in range(heads):
                value = arrived[z, c]
                pieces = [value[:, s * HEAD : (s + 1) * HEAD] for s in range(seqs)]
                lanes.append(jnp.concatenate(pieces, axis=0))
            attended.append(jnp.concatenate(lanes, axis=1))
        else:
            attended.append(arrived[z])
        right[k, :, 4 * features : 5 * features] = attended[k]
        right[k, :, 5 * features :] = jnp.zeros_like(right[k, :, 5 * features :])
    update = jnp.zeros_like(total)
    for k in range(tp):
        wait(k)
        update += mm(attended[k], narrow(store, k, features)[0])
    total = total + update
    after_row[...] = total
    low = layer_norm(total, gain[...]).astype(BF)
    normed[...] = low
    rule = same_column(count, few)
    update = jnp.zeros_like(total)
    for k in range(tp):
        weights = narrow(store, k, features)
        for t in range(3):
            proj[t, k] = mm_nt(low, weights[2 + t]).astype(BF)
        mixed = []
        for h in range(heads):
            at = slice(h * HEAD, (h + 1) * HEAD)
            probs = column_probs(proj[0, k, :, at], proj[1, k, :, at], rule, HEAD**-0.5)
            mixed.append(mm(probs.astype(BF), proj[2, k, :, at]).astype(BF))
        mixed = jnp.concatenate(mixed, axis=1)
        right[k, :, 3 * features : 4 * features] = mixed
        update += mm(mixed, weights[1])
    after_col[...] = total + update


def columns_backward(dims, parts, me_ref, *refs):
    few, tp, heads = dims
    middle, outputs, after_row, normed, proj, right, gain, shard = refs[:8]
    parts, refs = refs[8 : 8 + parts], refs[8 + parts :]
    home, left, right_out, row_mixed, gain_grad, store, sems = refs
    wait = fetch(me_ref, tp, shard, parts, store, sems)
    features = heads * HEAD
    count = middle.shape[0]
    seqs = count // few
    middle_low = middle[...].astype(BF)
    left[0] = normed[...]
    left[1] = middle_low
    rule = same_column(count, few)
    upstream = jnp.zeros(middle.shape, F32)
    for k in range(tp):
        wait(k)
        weights = narrow(store, k, features)
        mixed_grad = mm_nt(middle_low, weights[1]).astype(BF)
        grads = [[], [], []]
        for h in range(heads):
            at = slice(h * HEAD, (h + 1) * HEAD)
            query, key, value = proj[0, k, :, at], proj[1, k, :, at], proj[2, k, :, at]
            probs = column_probs(query, key, rule, HEAD**-0.5)
            out_grad = mixed_grad[:, at]
            prob_grad = mm_nt(out_grad, value)
            score = probs * (prob_grad - jnp.sum(probs * prob_grad, axis=-1, keepdims=True))
            score = score.astype(BF)
            grads[0].append((mm(score, key) * HEAD**-0.5).astype(BF))
            grads[1].append((mm(score.T, query) * HEAD**-0.5).astype(BF))
            grads[2].append(mm(probs.astype(BF).T, out_grad).astype(BF))
        for t in range(3):
            grad = jnp.concatenate(grads[t], axis=1)
            upstream += mm(grad, weights[2 + t])
            right_out[k, :, t * features : (t + 1) * features] = grad
        right_out[k, :, 3 * features :] = right[k, :, 3 * features :]
    back, gain_grad[...] = norm_back(after_row[...], gain[...], upstream)
    low = (middle[...] + back).astype(BF)
    home[:, 0] = outputs[...].reshape(seqs, few, -1)
    home[:, 1] = low.reshape(seqs, few, -1)
    left[2] = low
    for k in range(tp):
        z = me_ref[1] ^ k
        value = mm_nt(low, narrow(store, k, features)[0]).astype(BF)
        if len(row_mixed.shape) == 4:
            for c in range(heads):
                lane = value[:, c * HEAD : (c + 1) * HEAD]
                pieces = [lane[s * few : (s + 1) * few] for s in range(seqs)]
                row_mixed[z, c] = jnp.concatenate(pieces, axis=1)
            row_mixed[z, heads:] = jnp.zeros_like(row_mixed[z, heads:])
        else:
            row_mixed[z] = value


def store_halves(halves, z, value):
    rows = value.shape[0] // 2
    for half, part in zip(halves, (value[:rows], value[rows:])):
        half[:, z] = part.reshape(half.shape[0], half.shape[2], -1)


def column_weights(orders, me_ref, left, left_other, right, right_other, *refs):
    tp = right.shape[0]
    qkv, col_out, row_out, rows = refs[0:2], refs[2:4], refs[4:6], refs[6]
    features = col_out[0].shape[3]
    turned = []
    for i in range(3):
        value = jnp.concatenate([left[i], left_other[i]], axis=0).T
        turned.append(relative_rows(me_ref, orders[i], value, rows.at[i], 4))
    for k in range(tp):
        value = jnp.concatenate([right[k], right_other[k]], axis=0)
        start = 0
        for i, (halves, size) in enumerate(((qkv, 3), (col_out, 1), (row_out, 1))):
            columns = slice(start, start + size * features)
            store_halves(halves, me_ref[1] ^ k, mm(turned[i], value[:, columns]).astype(BF))
            start += size * features


def wide_weights(orders, me_ref, left, left_other, right, right_other, *refs):
    rows = refs[4]
    for i, grads in enumerate((refs[0:2], refs[2:4])):
        value = jnp.concatenate([left[i], left_other[i]], axis=0).T
        turned = relative_rows(me_ref, orders[i], value, rows.at[i], 4)
        for k in range(right.shape[1]):
            both = jnp.concatenate([right[i, k], right_other[i, k]], axis=0)
            store_halves(grads, me_ref[1] ^ k, mm(turned, both).astype(BF))


def feed_forward(tp, parts, me_ref, after_col, arrived, gain, up_shard, down_shard, *refs):
    parts, refs = refs[:parts], refs[parts:]
    outputs, middle, gain_grad, left, right, store, sems = refs
    half = store.shape[1] // 2
    own = [
        pltpu.make_async_copy(up_shard, store.at[0, pl.ds(0, half)], sems.at[0, 0]),
        pltpu.make_async_copy(down_shard, store.at[0, pl.ds(half, half)], sems.at[0, 1]),
    ]
    wait = shard_copies(me_ref, tp, own, parts, store, sems)
    value = after_col[...]
    low = layer_norm(value, gain[...]).astype(BF)
    given = arrived[:, 1].reshape(value.shape)
    left[0] = low
    left[1] = given
    result = value
    upstream = jnp.zeros_like(value)
    for k in range(tp):
        wait(k)
        up = store[k, :half].reshape(-1, store.shape[3])
        down = store[k, half:].reshape(-1, store.shape[3])
        hidden, slope = gelu_parts(mm(low, up))
        hidden = hidden.astype(BF)
        right[1, k] = hidden
        result += mm(hidden, down)
        pre_grad = (mm_nt(given, down) * slope).astype(BF)
        right[0, k] = pre_grad
        upstream += mm_nt(pre_grad, up)
    outputs[...] = result.astype(BF)
    back, gain_grad[...] = norm_back(value, gain[...], upstream)
    middle[...] = given.astype(F32) + back


def gather_grads(dims, order, me_ref, back, normed, gain, weight, *outs):
    slots, ranks, few, tp, heads = dims
    features = heads * HEAD
    part = slots * few
    pieces, kept, sent, gain_grad, rows = outs
    total = jnp.zeros((3 * features, normed.shape[2]), F32)
    for k in range(tp):
        z = me_ref[1] ^ k
        columns = pl.ds(pl.multiple_of(z * part, part), part)
        for c in range(heads):
            for r in range(ranks):
                for t in range(3):
                    piece = back[c * ranks + r, t, :, columns]
                    at = t * features + c * HEAD
                    pieces[z, at : at + HEAD, r * part : (r + 1) * part] = piece
        total += mm(pieces[z], normed[z])
    gain_grad[...] = (
        jnp.sum(total * weight[...].astype(F32), axis=0, keepdims=True) / gain[...]
    )
    turned = relative_rows(me_ref, order, total.T.astype(BF), rows)
    half = turned.shape[0] // 2
    kept[...] = turned[:half].reshape(kept.shape)
    sent[...] = turned[half:].reshape(sent.shape)


def finish(dims, parts, me_ref, *refs):
    slots, ranks, few, tp, heads = dims
    features = heads * HEAD
    pieces, tokens, gain, home, shard = refs[:5]
    parts, (result, store, sems) = refs[5 : 5 + parts], refs[5 + parts :]
    wait = fetch(me_ref, tp, shard, parts, store, sems)
    inner = home[:, few : 2 * few].reshape(tokens.shape)
    upstream = jnp.zeros(inner.shape, F32)
    for k in range(tp):
        wait(k)
        whole = store[k].reshape(-1, store.shape[3])[: 3 * features]
        upstream += mm(pieces[me_ref[1] ^ k].T, whole)
    upstream = upstream.reshape(ranks, slots, few, -1)
    upstream = jnp.concatenate(
        [upstream[r, c] for c in range(slots) for r in range(ranks)], axis=0
    )
    back, _ = norm_back(tokens[...].astype(F32), gain[...], upstream)
    result[...] = (inner.astype(F32) + back).astype(BF)


def after(value, *others):
    return lax.optimization_barrier((value,) + others)[0]


def together(*values):
    return lax.optimization_barrier(values)


def two_terms(gains):
    high = lax.reduce_precision(gains, 8, 7)
    low = gains - high
    return jnp.pad(jnp.concatenate([high, low], axis=0), ((0, 10), (0, 0))).astype(BF)


def one_term(rows):
    return rows[:3] + rows[3:6]


def add(left, right):
    return (left.astype(F32) + right.astype(F32)).astype(BF)


def local(
    tokens,
    cotangent,
    lengths,
    column_mask,
    row_gain,
    row_qkv,
    row_out,
    col_gain,
    col_qkv,
    col_out,
    ffn_gain,
    ffn_up,
    ffn_down,
):
    slots, ranks, tp = lax.axis_size("c"), lax.axis_size("r"), lax.axis_size("tp")
    seqs = slots * ranks
    block, width = tokens.shape[2], tokens.shape[3]
    cols = column_mask.shape[1]
    few = block // seqs
    part = slots * few
    features = row_qkv.shape[2]
    heads = features // HEAD
    hidden = ffn_up.shape[1]
    queries = tp * part
    count = seqs * few
    tied_scale = (HEAD * seqs) ** (-0.5)
    my_seq, my_rank, my_z = lax.axis_index(SEQ), lax.axis_index("r"), lax.axis_index("tp")
    me_ref = jnp.stack([my_seq, my_z]).astype(jnp.int32)
    dims = (slots, ranks, few, tp, heads)
    fast = seqs == 8 and ranks == 2
    row_gain, col_gain, ffn_gain = row_gain[None], col_gain[None], ffn_gain[None]

    penalty_scale = ENTROPY_WEIGHT * (seqs * cols) / (HEADS * jnp.sum(lengths).astype(F32))
    position = jnp.arange(cols, dtype=jnp.int32).reshape(tp, slots, ranks, few)
    position = position.transpose(2, 0, 1, 3)
    flag = column_mask.reshape(tp, slots, ranks, few).transpose(2, 0, 1, 3)
    valid = (position < lengths[0]) & ((flag == 1) | (position == 0))
    valid = valid.astype(F32).reshape(ranks, queries)
    key_ok = jnp.concatenate(
        [lax.dynamic_index_in_dim(valid, my_rank ^ k, 0) for k in range(ranks)], axis=1
    )
    query_position = lax.dynamic_index_in_dim(position.reshape(ranks, queries), my_rank, 0)
    query_weight = jnp.where(query_position < lengths[0], penalty_scale, 0.0).reshape(queries, 1)

    own = tokens[0, 0]
    both = [value.reshape(seqs, few, width) for value in (own, cotangent[0, 0])]
    both = jnp.stack(both, axis=1)

    row_weight = row_qkv.transpose(0, 2, 1).reshape(3 * features, width)
    shard_a = jnp.concatenate(
        [row_out, col_out, col_qkv.transpose(0, 2, 1).reshape(3 * features, width)]
    )

    def cut(shard, least):
        rows = shard.shape[0]
        rows += -rows % (seqs * least)
        shard = jnp.pad(shard, ((0, rows - shard.shape[0]), (0, 0)))
        return shard.reshape(seqs, rows // seqs, width)

    shard_a = cut(shard_a, 16 if fast else 1)
    shard_c = cut(row_weight, 16 if fast else 1)
    shard_b = cut(jnp.concatenate([ffn_up, ffn_down]), 1)

    def mine(shard):
        return lax.dynamic_index_in_dim(shard, my_seq, 0, keepdims=False)

    def along_tp(piece):
        return jnp.stack([swap(piece, "tp", tp, k) for k in range(1, tp)])

    def along_plane(held):
        return [swap(held, "c", slots, mask) for mask in (1, 2)]

    def across_plane(near):
        half = near[0].shape[1] // 2
        one = swap(near[0][:, :half], "c", slots, 2)
        return [one, swap(near[1][:, half:], "c", slots, 1)]

    def along_cores(parts):
        held = jnp.concatenate(parts, axis=1)
        return [held, swap(held, "r", ranks, 1)]

    def blocks_of(value):
        return [own] + [swap(value, "tp", tp, k) for k in range(1, tp)]

    if fast:
        near_a = along_tp(mine(shard_a))
        sent, both, near_a = together(own, both, near_a)
        blocks = blocks_of(sent)
        both = exchange(both, SEQ)
        plane_a = along_plane(near_a)
        blocks[1], blocks[2], blocks[3], both, *plane_a = together(*blocks[1:], both, *plane_a)
        near_b = along_tp(after(mine(shard_b), blocks[1]))
    else:
        blocks = blocks_of(own)
        both = exchange(both, SEQ)

        def everywhere(shard):
            rows = shard.shape[0] * shard.shape[1]
            whole = lax.all_gather(mine(shard), ("tp",) + SEQ, axis=0)
            return [whole.reshape(tp, 8, rows // 8, width)]

        parts_a, parts_b, parts_c = everywhere(shard_a), everywhere(shard_b), everywhere(shard_c)
        shard_a = shard_a.reshape(8, -1, width)
        shard_c = shard_c.reshape(8, -1, width)
    up_own = ffn_up.reshape(4, -1, width)
    down_own = ffn_down.reshape(4, -1, width)
    store_a = pltpu.VMEM((tp,) + shard_a.shape, BF)
    store_b = pltpu.VMEM((tp, 8, shard_b.shape[0] * shard_b.shape[1] // 8, width), BF)
    store_c = pltpu.VMEM((tp,) + shard_c.shape, BF)
    sems = pltpu.SemaphoreType.DMA((tp, 10))

    if fast:
        normed, pieces = call(
            functools.partial(project, dims),
            [((tp, block, width), BF), ((seqs, 3, HEAD, queries), BF)],
            me_ref,
            *blocks,
            row_gain,
            row_weight,
            specs=[SMEM] + [VMEM] * (tp + 2),
            flops=2 * cols * width * 3 * features,
            moved=8 << 20,
        )
    else:
        order = jnp.stack(blocks)[my_z ^ jnp.arange(tp)]
        order = order.reshape(tp, slots, ranks, few, width).transpose(0, 2, 1, 3, 4)
        normed = layer_norm(order.astype(F32), row_gain).astype(BF).reshape(tp, block, width)
        pieces = jnp.einsum("fd,zld->fzl", row_weight, normed, preferred_element_type=F32)
        pieces = pieces.astype(BF).reshape(3, heads, HEAD, tp, ranks, part)
        pieces = pieces.transpose(1, 4, 0, 2, 3, 5).reshape(heads, ranks, 3, HEAD, queries)
        pieces = jnp.pad(pieces, ((0, slots - heads),) + ((0, 0),) * 4)
        pieces = pieces.reshape(seqs, 3, HEAD, queries)
    if fast:
        pieces, *plane_a = together(pieces, *plane_a)
        cross_a = across_plane(plane_a)
    pieces = exchange(pieces, SEQ)
    mixed_shape = (tp * slots, few, seqs * HEAD)
    if fast:
        pieces, near_b, *cross_a = together(pieces, near_b, *cross_a)
        others = swap(pieces, "r", ranks, 1)
        others, near_b = together(others, near_b)
        plane_b = along_plane(near_b)
        parts_a = along_cores([near_a] + plane_a + cross_a)
        (mixed,) = call(
            functools.partial(attend, tied_scale),
            [(mixed_shape, BF)],
            pieces,
            others,
            key_ok,
            flops=4 * cols * queries * seqs * HEAD,
            moved=8 << 20,
        )
    else:
        pairs = lax.all_gather(pieces[:, 1:], "r", axis=0)
        pairs = pairs.transpose(2, 1, 3, 0, 4).reshape(2, seqs * HEAD, cols)
        key, value = pairs[0], pairs[1]
        query = pieces[:, 0].reshape(seqs * HEAD, queries)
        key_ok = valid.reshape(1, cols)
        logits = jnp.einsum("ki,kj->ij", query, key, preferred_element_type=F32) * tied_scale
        masked = jnp.where(key_ok > 0, logits, NEGATIVE)
        powers = jnp.exp(masked - jnp.max(masked, axis=-1, keepdims=True))
        probs = powers / jnp.sum(powers, axis=-1, keepdims=True)
        mixed = jnp.einsum("ij,kj->ik", probs.astype(BF), value, preferred_element_type=F32)
        mixed = mixed.astype(BF).reshape(mixed_shape)
    if fast:
        mixed, parts_a[1], *plane_b = together(mixed, parts_a[1], *plane_b)
        cross_b = across_plane(plane_b)
    mixed = exchange(mixed, ("tp", "c"))
    shards = (tp, count, features)
    if fast:
        mixed, *cross_b = together(mixed, *cross_b)
        arrived = mixed.reshape(tp, slots, few, seqs * HEAD)
        parts_b = along_cores([near_b] + plane_b + cross_b)
        near_c = along_tp(after(mine(shard_c), mixed))
    else:
        arrived = (
            mixed.reshape(tp, slots, few, seqs, HEAD)[:, :heads]
            .transpose(0, 3, 2, 1, 4)
            .reshape(shards)
        )

    flat = (count, width)
    packed = (tp, count, 5 * features + -5 * features % 128)
    n_parts = len(parts_a)
    after_row, col_normed, col_proj, col_right, after_col = call(
        functools.partial(columns_forward, (few, tp, heads), n_parts),
        [(flat, F32), (flat, BF), ((3,) + shards, BF), (packed, BF), (flat, F32)],
        me_ref,
        both,
        arrived,
        col_gain,
        shard_a,
        *parts_a,
        specs=[SMEM] + [VMEM] * 3 + [ANY] * (1 + n_parts),
        scratch=[store_a, sems],
        flops=2 * count * width * width * 5,
        moved=20 << 20,
    )
    if fast:
        after_col, near_c = together(after_col, near_c)
        plane_c = along_plane(near_c)
    outputs, middle, ffn_gain_grad, wide_left, wide_right = call(
        functools.partial(feed_forward, tp, n_parts),
        [
            (flat, BF),
            (flat, F32),
            ((1, width), F32),
            ((2,) + flat, BF),
            ((2, tp, count, hidden), BF),
        ],
        me_ref,
        after_col,
        both,
        ffn_gain,
        up_own,
        down_own,
        *parts_b,
        specs=[SMEM] + [VMEM] * 3 + [ANY] * (2 + n_parts),
        scratch=[store_b, sems],
        flops=2 * count * width * hidden * tp * 4,
        moved=30 << 20,
    )
    home, col_left, col_right, row_mixed, col_gain_grad = call(
        functools.partial(columns_backward, (few, tp, heads), n_parts),
        [
            ((seqs, 2, few, width), BF),
            ((3,) + flat, BF),
            (packed, BF),
            ((tp, slots, few, seqs * HEAD) if fast else shards, BF),
            ((1, width), F32),
        ],
        me_ref,
        middle,
        outputs,
        after_row,
        col_normed,
        col_proj,
        col_right,
        col_gain,
        shard_a,
        *parts_a,
        specs=[SMEM] + [VMEM] * 7 + [ANY] * (1 + n_parts),
        scratch=[store_a, sems],
        flops=2 * count * width * width * 8,
        moved=30 << 20,
    )

    def halve(kept, came):
        half = kept.shape[0] // 2
        return add(kept[:half], came[:half]), add(kept[half:], came[half:])

    def give(sent, mask):
        return swap(sent, "c", slots, mask)

    def last(held):
        return jnp.sum(exchange(held, "tp").astype(F32), axis=0)

    def all_at_once(left, right):
        grad = jnp.einsum("ld,zlf->zdf", left, right, preferred_element_type=F32).astype(BF)
        grad = lax.psum_scatter(grad, SEQ, scatter_dimension=1, tiled=True)
        return lax.psum_scatter(grad, "tp", scatter_dimension=0, tiled=True)[0].astype(F32)

    rows_of = width // seqs
    turned_rows = pltpu.VMEM((3, width, 2 * count), BF)
    if fast:
        wide_others = swap(wide_left, "r", ranks, 1), swap(wide_right, "r", ranks, 1)
        col_others = swap(col_left, "r", ranks, 1), swap(col_right, "r", ranks, 1)
        up_kept, up_sent, down_kept, down_sent = call(
            functools.partial(wide_weights, ((0, 2, 1), (0, 1, 2))),
            [((2, tp, rows_of, hidden), BF)] * 4,
            me_ref,
            wide_left,
            wide_others[0],
            wide_right,
            wide_others[1],
            specs=[SMEM] + [VMEM] * 4,
            scratch=[turned_rows],
            flops=2 * count * width * hidden * tp * 2,
            moved=30 << 20,
        )
        qkv_kept, qkv_sent, *outs_halves = call(
            functools.partial(column_weights, ((0, 2, 1), (0, 1, 2), (0, 1, 2))),
            [((2, tp, rows_of, 3 * features), BF)] * 2
            + [((2, tp, rows_of, features), BF)] * 4,
            me_ref,
            after(col_left, up_sent),
            col_others[0],
            col_right,
            col_others[1],
            specs=[SMEM] + [VMEM] * 4,
            scratch=[turned_rows],
            flops=2 * count * width * width * 5,
            moved=12 << 20,
        )
    else:
        row_mixed = row_mixed.reshape(tp, seqs, few, heads, HEAD).transpose(0, 3, 2, 1, 4)
        row_mixed = jnp.pad(row_mixed, ((0, 0), (0, slots - heads)) + ((0, 0),) * 3)
        my_order = my_z ^ jnp.arange(tp)
        col_right = col_right[my_order]
    row_mixed = exchange(row_mixed.reshape(mixed_shape), ("tp", "c"))
    if fast:
        up_sent, down_sent, *plane_c = together(up_sent, down_sent, *plane_c)
        up_came, down_came = give(up_sent, 2), give(down_sent, 1)
        row_mixed = after(row_mixed, qkv_sent)
        query_grad, kept, sent = call(
            functools.partial(attend_back, tied_scale),
            [
                ((seqs, HEAD, queries), BF),
                ((seqs, 2, HEAD, queries), F32),
                ((seqs, 2, HEAD, queries), BF),
            ],
            pieces,
            others,
            key_ok,
            query_weight,
            row_mixed,
            flops=10 * cols * queries * seqs * HEAD,
            moved=16 << 20,
        )
        sent = after(sent, up_came, down_came)
        pair_grad = (kept + swap(sent, "r", ranks, 1).astype(F32)).astype(BF)
        (up_kept, up_sent), (down_kept, down_sent) = halve(up_kept, up_came), halve(down_kept, down_came)
        up_came, down_came = give(up_sent, 1), give(down_sent, 2)
        back = jnp.concatenate([query_grad[:, None], pair_grad], axis=1)
        back, up_came, down_came = together(back, up_came, down_came)
        wide_last = jnp.concatenate(
            [add(up_kept, up_came)[0], add(down_kept, down_came)[0]], axis=-1
        )
        wide_came = [
            swap(lax.dynamic_index_in_dim(wide_last, my_z ^ k, keepdims=False), "tp", tp, k)
            for k in range(1, tp)
        ]
    else:
        out_grad = row_mixed.reshape(queries, seqs * HEAD)
        prob_grad = jnp.einsum("ik,kj->ij", out_grad, value, preferred_element_type=F32)
        prob_dot = jnp.sum(probs * prob_grad, axis=-1, keepdims=True)
        mean_logit = jnp.sum(
            jnp.where(key_ok > 0, probs * masked, 0.0), axis=-1, keepdims=True
        )
        entropy = jnp.where(key_ok > 0, probs * (masked - mean_logit), 0.0)
        grad = (probs * (prob_grad - prob_dot) - query_weight * entropy).astype(BF)
        total = jnp.einsum("ij,kj->ki", grad, key, preferred_element_type=F32)
        query_grad = (total * tied_scale).astype(BF).reshape(seqs, HEAD, queries)
        key_grad = jnp.einsum("ki,ij->kj", query, grad, preferred_element_type=F32)
        value_grad = jnp.einsum(
            "ik,ij->kj", out_grad, probs.astype(BF), preferred_element_type=F32
        )
        both = jnp.stack([(key_grad * tied_scale).astype(BF), value_grad.astype(BF)])
        both = both.reshape(2, seqs, HEAD, ranks, queries).transpose(3, 1, 0, 2, 4)
        pair_grad = lax.psum_scatter(both, "r", scatter_dimension=0, tiled=False)
        back = jnp.concatenate([query_grad[:, None], pair_grad], axis=1)
    back = exchange(back, SEQ)
    if fast:
        col_out_kept, col_out_sent, row_out_kept, row_out_sent = outs_halves
        outs_kept = jnp.concatenate([col_out_kept, row_out_kept], axis=3)
        outs_sent = jnp.concatenate([col_out_sent, row_out_sent], axis=3)
        qkv_sent, outs_sent, back, *rest = together(qkv_sent, outs_sent, back, *plane_c, *wide_came)
        plane_c, wide_came = rest[:2], rest[2:]
        qkv_came, outs_came = give(qkv_sent, 2), give(outs_sent, 1)
        wide_grad = lax.dynamic_index_in_dim(wide_last, my_z, keepdims=False).astype(F32)
        for value in wide_came:
            wide_grad = wide_grad + value.astype(F32)
        parts_c = along_cores([near_c] + plane_c + across_plane(plane_c))
        traded, kept, sent, row_gain_grad = call(
            functools.partial(gather_grads, dims, (0, 2, 1)),
            [((tp, 3 * features, block), BF)]
            + [((4, rows_of, 3 * features), BF)] * 2
            + [((1, width), F32)],
            me_ref,
            back,
            normed,
            row_gain,
            row_weight,
            specs=[SMEM] + [VMEM] * 4,
            scratch=[pltpu.VMEM((width, 3 * features), BF)],
            flops=2 * cols * width * 3 * features,
            moved=8 << 20,
        )
    else:
        both = back.reshape(slots, ranks, 3, HEAD, tp, part)[:heads]
        both = both.transpose(4, 2, 0, 3, 1, 5).reshape(tp, 3 * features, block)
        row_grad = jnp.einsum("zld,zfl->df", normed, both, preferred_element_type=F32)
        row_gain_grad = (
            jnp.sum(row_grad.T * row_weight.astype(F32), axis=0, keepdims=True) / row_gain
        )
        traded = both
    gains = jnp.concatenate([row_gain_grad, col_gain_grad, ffn_gain_grad], axis=0)
    home = home.reshape(seqs, 2 * few, width)
    if fast:
        traded, qkv_came, outs_came = together(traded, qkv_came, outs_came)
        traded = exchange(traded, "tp")
        (qkv_kept, qkv_sent), (outs_kept, outs_sent) = halve(qkv_kept, qkv_came), halve(outs_kept, outs_came)
        qkv_came, outs_came = give(qkv_sent, 1), give(outs_sent, 2)
        came = swap(sent, "r", ranks, 1)
        home, traded, qkv_came, outs_came, came = together(home, traded, qkv_came, outs_came, came)
        ends = jnp.broadcast_to(two_terms(gains), (seqs, 16, width))
        home = exchange(jnp.concatenate([home, ends], axis=1), SEQ)
        gains = one_term(jnp.sum(home[:, 2 * few :].astype(F32), axis=0))
        kept, sent = add(kept[:2], came[:2]), add(kept[2:], came[2:])
        kept, sent = halve(kept, give(sent, 2))
        row_grad = add(kept[0], give(sent, 1)[0]).astype(F32)
        small = jnp.concatenate(
            [add(qkv_kept, qkv_came)[0], add(outs_kept, outs_came)[0]], axis=-1
        )
        ends = jnp.pad(two_terms(gains), ((0, 0), (0, small.shape[2] - width)))
        ends = jnp.broadcast_to(ends, (tp,) + ends.shape)
        small = last(jnp.concatenate([small, ends], axis=1))
        gains = one_term(small[rows_of:, :width])
        small = small[:rows_of]
        qkv, outs = small[:, : 3 * features], small[:, 3 * features :]
        up_grad, down_grad = wide_grad[:, :hidden], wide_grad[:, hidden:]
    else:
        traded = exchange(traded, "tp")
        home = exchange(home, SEQ)
        for axis, size in (("r", ranks), ("c", slots), ("tp", tp)):
            for k in bits_of(size):
                gains = gains + swap(gains, axis, size, k)
    outputs = home[:, :few].reshape(block, width)
    (input_grad,) = call(
        functools.partial(finish, dims, n_parts),
        [((block, width), BF)],
        me_ref,
        traded,
        own,
        row_gain,
        home,
        shard_c,
        *parts_c,
        specs=[SMEM] + [VMEM] * 4 + [ANY] * (1 + n_parts),
        scratch=[store_c, sems],
        flops=2 * block * width * width * 3,
        moved=8 << 20,
    )
    if not fast:
        row_grad = lax.psum_scatter(row_grad, SEQ, scatter_dimension=0, tiled=True)
        wide_right = wide_right[:, my_order]
        up_grad = all_at_once(wide_left[0], wide_right[0])
        down_grad = all_at_once(wide_left[1], wide_right[1])
        qkv = all_at_once(col_left[0], col_right[..., : 3 * features])
        outs = jnp.concatenate(
            [
                all_at_once(col_left[1], col_right[..., 3 * features : 4 * features]),
                all_at_once(col_left[2], col_right[..., 4 * features : 5 * features]),
            ],
            axis=1,
        )

    def thirds(value):
        return value.reshape(width // seqs, 3, features).transpose(1, 0, 2)

    return (
        outputs[None, None],
        input_grad[None, None],
        gains[0],
        thirds(row_grad),
        outs[:, features:].T,
        gains[1],
        thirds(qkv),
        outs[:, :features].T,
        gains[2],
        up_grad,
        down_grad.T,
    )


def solution(mesh):
    seqs, tp = mesh.shape["seq"], mesh.shape["tp"]
    heads = HEADS // tp
    slots = 1 << (heads - 1).bit_length()
    split = Mesh(mesh.devices.reshape(slots, seqs // slots, tp), ("c", "r", "tp"))
    return jax.shard_map(
        local,
        mesh=split,
        in_specs=(
            P(None, SEQ, "tp", None),
            P(None, SEQ, "tp", None),
            P(),
            P(),
            P(),
            P(None, None, "tp"),
            P("tp", None),
            P(),
            P(None, None, "tp"),
            P("tp", None),
            P(),
            P(None, "tp"),
            P("tp", None),
        ),
        out_specs=(
            P(None, SEQ, "tp", None),
            P(None, SEQ, "tp", None),
            P(),
            P(None, SEQ, "tp"),
            P("tp", SEQ),
            P(),
            P(None, SEQ, "tp"),
            P("tp", SEQ),
            P(),
            P(SEQ, "tp"),
            P("tp", SEQ),
        ),
        check_vma=False,
    )
```
